256 devices in a mesh: dp: 2 (over z_lo), row: 8 (over z_hi, core), col: 16 (over y, x).
Axes of the slice: x: 4, y: 4, z: 8 (z_hi: 4, z_lo: 2; z = z_hi * 2 + z_lo), core: 2. Of those that a mesh axis runs over, the one named last changes fastest.
Arguments:
- tokens: bfloat16 [2048, 4096], P(('dp', 'col'), 'row'), may hold values from -6 to 6
- w_in: bfloat16 [4096, 16384], P('row', 'col'), may hold values from -0.09375 to 0.09375
- w_out: bfloat16 [16384, 4096], P('col', 'row'), may hold values from -0.046875 to 0.046875
- out_grad: bfloat16 [2048, 4096], P(('dp', 'col'), 'row'), may hold values from -6 to 6
Outputs:
- output: bfloat16 [2048, 4096], P(('dp', 'col'), 'row')
- grad_x: bfloat16 [2048, 4096], P(('dp', 'col'), 'row')
- grad_w_in: bfloat16 [4096, 16, 1024], P('row', 'col', 'dp')
- grad_w_out: bfloat16 [16, 1024, 4096], P('col', 'dp', 'row')
The draws below stay inside these ranges and needn't reach their ends.
All inputs are finite; a program needn't handle non-finite values.
Results may differ from the reference program's by a relative error of at most 0.005.
Values may be sent and summed in bfloat16 or wider, within the bound.
A program may use at most 64 MiB of HBM per device.

```python
import math
import jax
import jax.numpy as jnp

D = 4096
FF = 16384
TOKENS = 2048
N_COL = 16


def block_levels(rng, extent, split, least, high):
    level, own = 1.0, jax.random.fold_in(rng, 6)
    for axis_at, parts in split:
        heights = jnp.exp(jax.random.uniform(jax.random.fold_in(own, axis_at), (parts,), jnp.float32, least / len(split), high / len(split)))
        level = level * jnp.repeat(heights, extent[axis_at] // parts).reshape([-1 if axis == axis_at else 1 for axis in range(len(extent))])
    return level


def normal_values(rng, shape, scale, most, split=(), kind=jnp.bfloat16):
    values = jax.random.normal(rng, shape, jnp.float32) * scale
    if len(split) > 0:
        values = block_levels(rng, shape, split, -0.22, 0.18) * values
    return jnp.clip(values, min=-most, max=most).astype(kind)


def setup_inputs(seed: int = 0) -> dict:
    key_of = jax.random.split(jax.random.key(seed), 5)
    return {
        "tokens": normal_values(key_of[0], (TOKENS, D), 1.0, 6.0, ((0, 32), (1, 8))),
        "w_in": normal_values(key_of[1], (D, FF), D ** -0.5, 0.09375, ((0, 8), (1, 16))),
        "w_out": normal_values(key_of[2], (FF, D), FF ** -0.5, 0.046875, ((0, 16), (1, 8))),
        "out_grad": normal_values(key_of[3], (TOKENS, D), 1.0, 6.0, ((0, 32), (1, 8))),
    }


def gelu_parts(pre):
    cdf = 0.5 * (1.0 + jax.scipy.special.erf(pre / math.sqrt(2.0)))
    pdf = jnp.exp(-0.5 * pre * pre) / math.sqrt(2.0 * math.pi)
    return (pre * cdf, cdf + pre * pdf)

def reference(tokens, w_in, w_out, out_grad):
    pre = jnp.dot(tokens, w_in, preferred_element_type=jnp.float32)
    act_value, slope = gelu_parts(pre)
    act = act_value.astype(jnp.bfloat16)
    output = jnp.dot(act, w_out, preferred_element_type=jnp.float32).astype(jnp.bfloat16)
    grad_act = jnp.dot(out_grad, w_out.T, preferred_element_type=jnp.float32)
    grad_pre = (grad_act * slope).astype(jnp.bfloat16)
    grad_x = jnp.dot(grad_pre, w_in.T, preferred_element_type=jnp.float32).astype(jnp.bfloat16)
    gw_in = jnp.dot(tokens.T, grad_pre, preferred_element_type=jnp.float32)
    gw_out = jnp.dot(act.T, out_grad, preferred_element_type=jnp.float32)
    grad_w_in = gw_in.astype(jnp.bfloat16).reshape(D, N_COL, FF // N_COL)
    grad_w_out = gw_out.astype(jnp.bfloat16).reshape(N_COL, FF // N_COL, D)
    return (output, grad_x, grad_w_in, grad_w_out)
```

```python
import math

import jax
import jax.numpy as jnp
from jax import lax
from jax.experimental import pallas as pl
from jax.experimental.pallas import tpu as pltpu
from jax.sharding import PartitionSpec as P

F32, BF = jnp.float32, jnp.bfloat16
MESH = pl.DeviceIdType.MESH
COPIES = 256


def gelu_parts(pre):
    cdf = 0.5 * (1.0 + lax.erf(pre * (1.0 / math.sqrt(2.0))))
    pdf = jnp.exp(-0.5 * pre * pre) * (1.0 / math.sqrt(2.0 * math.pi))
    return pre * cdf, cdf + pre * pdf


def dot(left, right, dims):
    return lax.dot_general(left, right, ((dims[:1], dims[1:]), ((), ())), preferred_element_type=F32)


def wrap(p):
    return lax.rem(p, 4)


class Links:
    def __init__(self, ssem, rsem):
        self.ssem, self.rsem, self.copies = ssem, rsem, []

    def make(self, n, src, dst, dev):
        return pltpu.make_async_remote_copy(
            src_ref=src,
            dst_ref=dst,
            send_sem=self.ssem.at[n],
            recv_sem=self.rsem.at[n],
            device_id=dev,
            device_id_type=MESH,
        )

    def push(self, src, dst, dev):
        copy = self.make(len(self.copies), src, dst, dev)
        copy.start()
        self.copies.append((copy, dev))
        return len(self.copies) - 1

    def recv(self, n, ref):
        self.make(n, ref, ref, self.copies[n][1]).wait_recv()

    def drain(self):
        for copy, _ in self.copies:
            copy.wait_send()


def part(ref, half):
    n = ref.shape[0] // 2
    return ref.at[pl.ds(half * n, n)]


class Gather:
    def __init__(self, links, slot, ring):
        self.links, self.slot, (self.p, self.left, self.right) = links, slot, ring

    def start(self):
        mine = self.slot(self.p)
        self.a = self.links.push(mine, mine, self.right)
        self.b = self.links.push(mine, mine, self.left)

    def relay(self):
        near = self.slot(wrap(self.p + 3))
        self.links.recv(self.a, near)
        near = part(near, 0)
        self.c = self.links.push(near, near, self.right)
        near = self.slot(wrap(self.p + 1))
        self.links.recv(self.b, near)
        near = part(near, 1)
        self.d = self.links.push(near, near, self.left)

    def finish(self):
        far = self.slot(wrap(self.p + 2))
        self.links.recv(self.c, part(far, 0))
        self.links.recv(self.d, part(far, 1))


class Reduce:
    def __init__(self, links, bufs, keep, own, ring):
        self.links, (self.p, self.left, self.right) = links, ring
        self.so, self.sr, self.sl, self.ro, self.rl, self.rr = [bufs.at[i] for i in range(6)]
        self.kr, self.kl, self.own = keep.at[0], keep.at[1], own
        self.n = own.shape[0] // 2

    def put(self, chunk):
        n = self.n
        self.so[...] = chunk(wrap(self.p + 2), 0, 2 * n).astype(BF)
        self.opposite()
        self.sr[pl.ds(n, n)] = chunk(wrap(self.p + 1), n, n).astype(BF)
        self.sl[pl.ds(0, n)] = chunk(wrap(self.p + 3), 0, n).astype(BF)
        self.direct()
        self.kr[...] = chunk(wrap(self.p + 1), 0, n)
        self.kl[...] = chunk(wrap(self.p + 3), n, n)
        self.own[...] = chunk(self.p, 0, 2 * n)

    def opposite(self):
        self.a = self.links.push(part(self.so, 0), part(self.ro, 0), self.right)
        self.b = self.links.push(part(self.so, 1), part(self.ro, 1), self.left)

    def direct(self):
        self.c = self.links.push(part(self.sr, 1), part(self.rl, 1), self.right)
        self.d = self.links.push(part(self.sl, 0), part(self.rr, 0), self.left)

    def combine(self):
        n = self.n
        self.links.recv(self.a, part(self.ro, 0))
        self.sr[pl.ds(0, n)] = (self.kr[...] + self.ro[pl.ds(0, n)].astype(F32)).astype(BF)
        self.e = self.links.push(part(self.sr, 0), part(self.rl, 0), self.right)
        self.links.recv(self.b, part(self.ro, 1))
        self.sl[pl.ds(n, n)] = (self.kl[...] + self.ro[pl.ds(n, n)].astype(F32)).astype(BF)
        self.f = self.links.push(part(self.sl, 1), part(self.rr, 1), self.left)

    def arrive(self):
        self.links.recv(self.c, part(self.rl, 1))
        self.links.recv(self.d, part(self.rr, 0))
        self.links.recv(self.e, part(self.rl, 0))
        self.links.recv(self.f, part(self.rr, 1))

    def total(self, *at):
        return self.own[at] + self.rl[at].astype(F32) + self.rr[at].astype(F32)


def kernel(
    tok, w_in, w_out, og,
    out_o, gx_o, gwi_o, gwo_o,
    X, XO, G, GO, win, wino, wout, wouto,
    Act, Pg, zb, zk, zw, slope,
    O, b1, k1, w1, b2, k2, w2, sd, rd, acco, acci,
    lsem, ssem, rsem,
):
    d, row, col = lax.axis_index("dp"), lax.axis_index("row"), lax.axis_index("col")
    k, c = lax.div(row, 2), lax.rem(row, 2)
    y, x = lax.div(col, 4), lax.rem(col, 4)
    core = {"row": 2 * k + (1 - c)}
    twin = {"dp": 1 - d}
    zring = (k, {"row": 2 * wrap(k + 3) + c}, {"row": 2 * wrap(k + 1) + c})
    yring = (y, {"col": 4 * wrap(y + 3) + x}, {"col": 4 * wrap(y + 1) + x})
    xring = (x, {"col": 4 * y + wrap(x + 3)}, {"col": 4 * y + wrap(x + 1)})
    links = Links(ssem, rsem)

    local = [
        pltpu.make_async_copy(tok, X.at[:, y, x, d], lsem.at[0]),
        pltpu.make_async_copy(og, G.at[:, y, x, d], lsem.at[1]),
        pltpu.make_async_copy(w_out.at[d], wout, lsem.at[2]),
        pltpu.make_async_copy(w_in.at[:, pl.ds(pl.multiple_of(d * 512, 512), 256)], win.at[0], lsem.at[3]),
        pltpu.make_async_copy(w_in.at[:, pl.ds(pl.multiple_of(d * 512 + 256, 256), 256)], win.at[1], lsem.at[4]),
    ]
    for copy in local:
        copy.start()
    barrier = pltpu.get_barrier_semaphore()
    for dev in (core, twin, zring[1], zring[2], yring[1], yring[2], xring[1], xring[2]):
        pl.semaphore_signal(barrier, inc=1, device_id=dev, device_id_type=MESH)
    pl.semaphore_wait(barrier, 8)

    js = (wrap(k + 2), wrap(k + 1), wrap(k + 3), k)
    twins, first, second, shared = [], [[], []], [[], []], [[], []]
    for copy, full in zip(local[:2], (X, G)):
        copy.wait()
        mine = full.at[:, y, x, d]
        twins.append(links.push(mine, mine, twin))
    for copy in local[2:]:
        copy.wait()
    w_swap = (
        links.push(win.at[1 - c], wino, core),
        links.push(wout.at[1 - c], wouto, core),
    )

    def begin(a, full):
        links.recv(twins[a], full.at[:, y, x, 1 - d])
        for i in range(4):
            j = js[i]
            if i % 2 == 0:
                one = Gather(links, lambda p, j=j: full.at[j, y, p], xring)
                two = Gather(links, lambda p, j=j: full.at[j, p], yring)
            else:
                one = Gather(links, lambda p, j=j: full.at[j, p, x], yring)
                two = Gather(links, lambda p, j=j: full.at[j, :, p], xring)
            first[a].append(one)
            second[a].append(two)
            one.start()

    def share(a, i, full, other, p):
        ref = second[a][i].slot(p)
        to = other.at[js[i], p] if i % 2 == 0 else other.at[js[i], :, p]
        shared[a].append((i, links.push(ref, to, core), to))

    def widen(a, i, full, other):
        first[a][i].finish()
        second[a][i].start()
        share(a, i, full, other, second[a][i].p)

    def widen_relay(a, i, full, other):
        second[a][i].relay()
        share(a, i, full, other, wrap(second[a][i].p + 3))
        share(a, i, full, other, wrap(second[a][i].p + 1))

    def widen_finish(a, i, full, other):
        second[a][i].finish()
        share(a, i, full, other, wrap(second[a][i].p + 2))

    def arrived(a, i):
        for at, n, to in shared[a]:
            if at == i:
                links.recv(n, to)

    def project(a, i, reduce):
        arrived(a, i)
        j = js[i]
        full, other, near, far, dims = ((X, XO, win, wino, (1, 0)), (G, GO, wout, wouto, (1, 1)))[a]
        for t in range(2):
            rows = pl.ds(2 * t, 2)
            value = dot(full[j, rows].reshape(256, 512), near[c], dims) + dot(
                other[j, rows].reshape(256, 512), far[...], dims
            )
            if i == 0:
                reduce.so[t] = value.astype(BF)
            elif i == 1 and t == 0:
                reduce.kr[0] = value
            elif i == 1:
                reduce.sr[1] = value.astype(BF)
            elif i == 2 and t == 0:
                reduce.sl[0] = value.astype(BF)
            elif i == 2:
                reduce.kl[0] = value
            else:
                reduce.own[t] = value
        if i == 0:
            reduce.opposite()
        if i == 2:
            reduce.direct()

    zred = [Reduce(links, zb.at[a], zk.at[a], zw.at[a], zring) for a in range(2)]
    begin(0, X)
    for i in range(4):
        first[0][i].relay()
    for i in range(4):
        widen(0, i, X, XO)
    begin(1, G)
    for i in range(4):
        widen_relay(0, i, X, XO)
    for i in range(4):
        first[1][i].relay()
    for i in range(4):
        widen_finish(0, i, X, XO)
    for i in range(4):
        widen(1, i, G, GO)
    links.recv(w_swap[0], wino)
    links.recv(w_swap[1], wouto)
    for i in range(4):
        project(0, i, zred[0])
    for i in range(4):
        widen_relay(1, i, G, GO)
    for i in range(4):
        widen_finish(1, i, G, GO)
    zred[0].combine()
    for i in range(4):
        project(1, i, zred[1])

    hidden = [Gather(links, lambda p: Act.at[c, p], zring), Gather(links, lambda p: Pg.at[c, p], zring)]
    spread = [{}, {}]

    def spread_to(a, j, b):
        full = (Act, Pg)[a]
        spread[a][b] = links.push(full.at[c, j], full.at[c, j], core)

    blocks = (k, wrap(k + 3), wrap(k + 1), wrap(k + 2))

    zred[0].arrive()
    for hh in range(2):

        @pl.loop(0, 8)
        def _(r):
            rows = pl.ds(pl.multiple_of(r * 32, 32), 32)
            act, gain = gelu_parts(zred[0].total(hh, rows))
            Act[c, k, hh, rows] = act.astype(BF)
            slope[hh, rows] = gain

    hidden[0].start()
    spread_to(0, k, 0)
    zred[1].combine()
    zred[1].arrive()
    for hh in range(2):

        @pl.loop(0, 8)
        def _(r):
            rows = pl.ds(pl.multiple_of(r * 32, 32), 32)
            Pg[c, k, hh, rows] = (zred[1].total(hh, rows) * slope[hh, rows]).astype(BF)

    hidden[1].start()
    spread_to(1, k, 0)

    plane = {}

    def rings(a, b):
        return (yring, xring) if (a + b) % 2 == 0 else (xring, yring)

    def emit(a, b):
        j, n = blocks[b], 4 * a + b
        full = (Act, Pg)[a]
        links.recv(spread[a][b], full.at[1 - c, j])
        for t in range(2):
            if a == 0:
                value = dot(Act[0, j, t], wout[0], (1, 0)) + dot(Act[1, j, t], wout[1], (1, 0))
            else:
                value = dot(Pg[0, j, t], win[0], (1, 1)) + dot(Pg[1, j, t], win[1], (1, 1))
            O[pl.ds(2 * t, 2)] = value.reshape(2, 4, 2, 16, 512)
        plane[a, b] = [Reduce(links, b1.at[n], k1.at[n], w1.at[n], rings(a, b)[0])]
        if (a + b) % 2 == 0:
            plane[a, b][0].put(lambda p, at, size: O[p, pl.ds(at, size)])
        else:
            plane[a, b][0].put(lambda p, at, size: O[pl.ds(at, size), p])

    def weights(a, b):
        j = blocks[b]
        for h in range(2):
            value = None
            for t in range(2):
                rows = pl.ds(2 * t, 2)
                if a == 0:
                    term = dot(Act[h, j, t], G[j, rows].reshape(256, 512), (0, 0))
                else:
                    term = dot(X[j, rows].reshape(256, 512), Pg[h, j, t], (0, 0))
                value = term if value is None else value + term
            acc = (acco, acci)[a]
            if b > 0:
                value = value + acc[h]
            if b < 3:
                acc[h] = value
            elif a == 0:
                gwo_o[h] = value.astype(BF)
            else:
                gwi_o[:, h * 256 : (h + 1) * 256] = value.astype(BF)

    def combine(a, b):
        plane[a, b][-1].combine()

    def narrow(a, b):
        n, one = 4 * a + b, plane[a, b][0]
        one.arrive()
        two = Reduce(links, b2.at[n], k2.at[n], w2.at[n], rings(a, b)[1])
        plane[a, b].append(two)
        two.put(lambda p, at, size: one.total(p, pl.ds(at, size)))

    def pair(a, b):
        n, two = 4 * a + b, plane[a, b][1]
        two.arrive()
        sd[n] = two.total(1 - d)
        plane[a, b].append(links.push(sd.at[n], rd.at[n], twin))

    def close(a, b):
        n = 4 * a + b
        links.recv(plane[a, b][2], rd.at[n])
        (out_o, gx_o)[a][blocks[b]] = (plane[a, b][1].total(d) + rd[n]).astype(BF)

    def relay(a):
        hidden[a].relay()
        spread_to(a, blocks[1], 1)
        spread_to(a, blocks[2], 2)

    def finish(a):
        hidden[a].finish()
        spread_to(a, blocks[3], 3)

    emit(0, 0), emit(1, 0)
    weights(0, 0)
    combine(0, 0), combine(1, 0)
    weights(1, 0)
    narrow(0, 0), narrow(1, 0)
    relay(0)
    emit(0, 1), emit(0, 2)
    combine(0, 0), combine(1, 0)
    weights(0, 1)
    combine(0, 1), combine(0, 2)
    weights(0, 2)
    pair(0, 0), pair(1, 0)
    relay(1)
    emit(1, 1), emit(1, 2)
    narrow(0, 1), narrow(0, 2)
    weights(1, 1)
    combine(1, 1), combine(1, 2)
    combine(0, 1), combine(0, 2)
    weights(1, 2)
    close(0, 0), close(1, 0)
    finish(0)
    emit(0, 3)
    narrow(1, 1), narrow(1, 2)
    pair(0, 1), pair(0, 2)
    combine(0, 3)
    finish(1)
    emit(1, 3)
    weights(0, 3)
    combine(1, 1), combine(1, 2)
    narrow(0, 3)
    combine(1, 3)
    weights(1, 3)
    pair(1, 1), pair(1, 2)
    combine(0, 3)
    narrow(1, 3)
    pair(0, 3)
    combine(1, 3)
    close(0, 1), close(0, 2), close(1, 1), close(1, 2), close(0, 3)
    pair(1, 3)
    close(1, 3)
    links.drain()


def on_device(tokens, w_in, w_out, out_grad):
    any_spec = pl.BlockSpec(memory_space=pl.ANY)
    vmem = pl.BlockSpec(memory_space=pltpu.VMEM)
    full = pltpu.VMEM((4, 4, 4, 2, 16, 512), BF)
    hid = pltpu.VMEM((2, 4, 2, 256, 256), BF)
    output, grad_x, gw_in, gw_out = pl.pallas_call(
        kernel,
        out_shape=(
            jax.ShapeDtypeStruct((4, 16, 512), BF),
            jax.ShapeDtypeStruct((4, 16, 512), BF),
            jax.ShapeDtypeStruct((512, 512), BF),
            jax.ShapeDtypeStruct((2, 256, 512), BF),
        ),
        in_specs=[any_spec] * 4,
        out_specs=(vmem,) * 4,
        scratch_shapes=[
            full, full, full, full,
            pltpu.VMEM((2, 512, 256), BF),
            pltpu.VMEM((512, 256), BF),
            pltpu.VMEM((2, 256, 512), BF),
            pltpu.VMEM((256, 512), BF),
            hid, hid,
            pltpu.VMEM((2, 6, 2, 256, 256), BF),
            pltpu.VMEM((2, 2, 1, 256, 256), F32),
            pltpu.VMEM((2, 2, 256, 256), F32),
            pltpu.VMEM((2, 256, 256), F32),
            pltpu.VMEM((4, 4, 2, 16, 512), F32),
            pltpu.VMEM((8, 6, 4, 2, 16, 512), BF),
            pltpu.VMEM((8, 2, 2, 2, 16, 512), F32),
            pltpu.VMEM((8, 4, 2, 16, 512), F32),
            pltpu.VMEM((8, 6, 2, 16, 512), BF),
            pltpu.VMEM((8, 2, 1, 16, 512), F32),
            pltpu.VMEM((8, 2, 16, 512), F32),
            pltpu.VMEM((8, 16, 512), F32),
            pltpu.VMEM((8, 16, 512), F32),
            pltpu.VMEM((2, 256, 512), F32),
            pltpu.VMEM((2, 512, 256), F32),
            pltpu.SemaphoreType.DMA((5,)),
            pltpu.SemaphoreType.DMA((COPIES,)),
            pltpu.SemaphoreType.DMA((COPIES,)),
        ],
        compiler_params=pltpu.CompilerParams(
            collective_id=0, has_side_effects=True, vmem_limit_bytes=58 << 20
        ),
        name="ffn",
    )(
        tokens.reshape(4, 16, 512),
        w_in,
        w_out.reshape(2, 2, 256, 512),
        out_grad.reshape(4, 16, 512),
    )
    return (
        output.reshape(64, 512),
        grad_x.reshape(64, 512),
        gw_in.reshape(512, 1, 512),
        gw_out.reshape(1, 512, 512),
    )


def solution(mesh):
    placed = (P(("dp", "col"), "row"), P("row", "col"), P("col", "row"), P(("dp", "col"), "row"))
    return jax.shard_map(
        on_device,
        mesh=mesh,
        in_specs=placed,
        out_specs=(
            P(("dp", "col"), "row"),
            P(("dp", "col"), "row"),
            P("row", "col", "dp"),
            P("col", "dp", "row"),
        ),
        check_vma=False,
    )
```

```python
import math

import jax
import jax.numpy as jnp
from jax import lax
from jax.experimental import pallas as pl
from jax.experimental.pallas import tpu as pltpu
from jax.sharding import PartitionSpec as P

F32, BF = jnp.float32, jnp.bfloat16
MESH = pl.DeviceIdType.MESH
SENDS, RECVS = 59, 91


def gelu_parts(pre):
    cdf = 0.5 * (1.0 + lax.erf(pre * (1.0 / math.sqrt(2.0))))
    pdf = jnp.exp(-0.5 * pre * pre) * (1.0 / math.sqrt(2.0 * math.pi))
    return pre * cdf, cdf + pre * pdf


def dot(left, right, dims):
    return lax.dot_general(left, right, ((dims[:1], dims[1:]), ((), ())), preferred_element_type=F32)


def wrap(p):
    return lax.rem(p, 4)


class Links:
    def __init__(self, ssem, rsem):
        self.ssem, self.rsem, self.sent, self.got, self.dev = ssem, rsem, [], 0, None

    def make(self, send, recv, src, dst, dev):
        return pltpu.make_async_remote_copy(
            src_ref=src,
            dst_ref=dst,
            send_sem=self.ssem.at[send],
            recv_sem=self.rsem.at[recv],
            device_id=dev,
            device_id_type=MESH,
        )

    def sends(self, total):
        self.sent.append(total)
        return len(self.sent) - 1

    def recvs(self):
        self.got += 1
        return self.got - 1

    def push(self, src, dst, dev, send=None, recv=None):
        send = self.sends(src) if send is None else send
        recv = self.recvs() if recv is None else recv
        self.make(send, recv, src, dst, dev).start()
        self.dev = dev
        return recv

    def recv(self, n, ref):
        self.make(0, n, ref, ref, self.dev).wait_recv()

    def drain(self):
        for n, total in enumerate(self.sent):
            self.make(n, 0, total, total, self.dev).wait_send()


def part(ref, half):
    n = ref.shape[0] // 2
    return ref.at[pl.ds(half * n, n)]


class Gather:
    def __init__(self, links, slot, ring, total):
        self.links, self.slot, (self.p, self.left, self.right) = links, slot, ring
        self.send, self.c = links.sends(total), links.recvs()

    def start(self):
        mine = self.slot(self.p)
        self.a = self.links.push(mine, mine, self.right, self.send)
        self.b = self.links.push(mine, mine, self.left, self.send)

    def relay(self):
        near = self.slot(wrap(self.p + 3))
        self.links.recv(self.a, near)
        near = part(near, 0)
        self.links.push(near, near, self.right, self.send, self.c)
        near = self.slot(wrap(self.p + 1))
        self.links.recv(self.b, near)
        near = part(near, 1)
        self.links.push(near, near, self.left, self.send, self.c)

    def finish(self):
        self.links.recv(self.c, self.slot(wrap(self.p + 2)))


class Direct:
    def __init__(self, links, ring, col, dp, twins):
        self.links, self.p, self.sent = links, ring, {}
        self.to = {}
        for r in range(4):
            for dd in range(2 if twins else 1):
                if r + dd > 0:
                    dev = {"col": col(wrap(ring + r))}
                    if dd == 1:
                        dev = {"dp": 1 - dp} if r == 0 else {**dev, "dp": 1 - dp}
                    self.to[r, dd] = dev

    def push(self, key, src, dst, send, recv=None):
        self.sent[key] = self.links.push(src, dst, self.to[key], send, recv)

    def recv(self, key, ref):
        self.links.recv(self.sent[key], ref)


class Reduce:
    def __init__(self, links, bufs, keep, own, ring):
        self.links, (self.p, self.left, self.right) = links, ring
        self.so, self.sr, self.sl, self.ro, self.rl, self.rr = [bufs.at[i] for i in range(6)]
        self.kr, self.kl, self.own, self.both = keep.at[0], keep.at[1], own, bufs.at[pl.ds(4, 2)]
        self.n = own.shape[0] // 2
        self.send, self.c = links.sends(bufs.at[pl.ds(0, 3)]), links.recvs()

    def opposite(self):
        self.a = self.links.push(part(self.so, 0), part(self.ro, 0), self.right, self.send)
        self.b = self.links.push(part(self.so, 1), part(self.ro, 1), self.left, self.send)

    def direct(self):
        self.links.push(part(self.sr, 1), part(self.rl, 1), self.right, self.send, self.c)
        self.links.push(part(self.sl, 0), part(self.rr, 0), self.left, self.send, self.c)

    def combine(self):
        n = self.n
        self.links.recv(self.a, part(self.ro, 0))
        self.sr[pl.ds(0, n)] = (self.kr[...] + self.ro[pl.ds(0, n)].astype(F32)).astype(BF)
        self.links.push(part(self.sr, 0), part(self.rl, 0), self.right, self.send, self.c)
        self.links.recv(self.b, part(self.ro, 1))
        self.sl[pl.ds(n, n)] = (self.kl[...] + self.ro[pl.ds(n, n)].astype(F32)).astype(BF)
        self.links.push(part(self.sl, 1), part(self.rr, 1), self.left, self.send, self.c)

    def arrive(self):
        self.links.recv(self.c, self.both)

    def total(self, *at):
        return self.own[at] + self.rl[at].astype(F32) + self.rr[at].astype(F32)


def kernel(
    tok, w_in, w_out, og,
    out_o, gx_o, gwi_o, gwo_o,
    X, XO, G, GO, win, wino, wout, wouto,
    Act, Pg, zb, zk, zw, slope,
    O, b1, w1, b2, w2, acco, acci,
    lsem, ssem, rsem,
):
    d, row, col = lax.axis_index("dp"), lax.axis_index("row"), lax.axis_index("col")
    k, c = lax.div(row, 2), lax.rem(row, 2)
    y, x = lax.div(col, 4), lax.rem(col, 4)
    core = {"row": 2 * k + (1 - c)}
    zring = (k, {"row": 2 * wrap(k + 3) + c}, {"row": 2 * wrap(k + 1) + c})
    links = Links(ssem, rsem)

    def xdirect(twins):
        return Direct(links, x, lambda p: 4 * y + p, d, twins)

    def ydirect(twins):
        return Direct(links, y, lambda p: 4 * p + x, d, twins)

    local = [
        pltpu.make_async_copy(tok, X.at[:, y, x, d], lsem.at[0]),
        pltpu.make_async_copy(og, G.at[:, y, x, d], lsem.at[1]),
        pltpu.make_async_copy(w_out.at[d], wout, lsem.at[2]),
        pltpu.make_async_copy(w_in.at[:, pl.ds(pl.multiple_of(d * 512, 512), 256)], win.at[0], lsem.at[3]),
        pltpu.make_async_copy(w_in.at[:, pl.ds(pl.multiple_of(d * 512 + 256, 256), 256)], win.at[1], lsem.at[4]),
    ]
    for copy in local:
        copy.start()
    barrier = pltpu.get_barrier_semaphore()
    peers = [core, zring[1], zring[2], *xdirect(True).to.values()]
    peers += [dev for (r, _), dev in ydirect(True).to.items() if r > 0]
    for dev in peers:
        pl.semaphore_signal(barrier, inc=1, device_id=dev, device_id_type=MESH)
    pl.semaphore_wait(barrier, len(peers))

    js = (wrap(k + 2), wrap(k + 1), wrap(k + 3), k)
    first, second, shares = {}, {}, {}

    def units(a, i):
        if a + i == 0:
            return [(0, slice(0, 256)), (1, slice(256, 512))]
        return [((a + i) % 2, slice(0, 512))]

    def begin(a, i):
        full, j = (X, G)[a], js[i]
        for turn, cols in units(a, i):
            first[a, i, turn] = one = (xdirect, ydirect)[turn](True)
            mine = full.at[j, y, x, d, :, cols]
            send, recv = links.sends(b2.at[8, pl.ds(0, 7), 0, :, cols]), links.recvs()
            for key in sorted(one.to, key=lambda key: (key[0] == 2, key)):
                one.push(key, mine, mine, send, recv)

    def share(a, i, turn, cols, p):
        j = js[i]
        ref, to = [
            (f.at[j, p, :, :, :, cols], f.at[j, :, p, :, :, cols])[turn] for f in ((X, XO), (G, GO))[a]
        ]
        if (a, i) not in shares:
            shares[a, i] = (links.sends((X, G)[a].at[j]), links.recvs())
        links.push(ref, to, core, *shares[a, i])

    def widen(a, i):
        full, j = (X, G)[a], js[i]
        for turn, cols in units(a, i):
            one = first[a, i, turn]
            one.recv((2, 1), b2.at[8, pl.ds(0, 7), 0, :, cols])
            second[a, i, turn] = two = (ydirect, xdirect)[turn](False)
            mine = (full.at[j, y, :, :, :, cols], full.at[j, :, x, :, :, cols])[turn]
            send = links.sends(full.at[j, pl.ds(0, 3), :, :, :, cols])
            for r in (1, 3, 2):
                two.push((r, 0), mine, mine, send)
        for turn, cols in units(a, i):
            share(a, i, turn, cols, second[a, i, turn].p)

    def widen_finish(a, i):
        full, j = (X, G)[a], js[i]
        for r in (1, 3, 2):
            for turn, cols in units(a, i):
                two = second[a, i, turn]
                p = wrap(two.p + 4 - r)
                two.recv((r, 0), (full.at[j, p, :, :, :, cols], full.at[j, :, p, :, :, cols])[turn])
                share(a, i, turn, cols, p)

    def project(a, i, reduce):
        j = js[i]
        links.recv(shares[a, i][1], (XO, GO)[a].at[j])
        full, other, near, far, dims = ((X, XO, win, wino, (1, 0)), (G, GO, wout, wouto, (1, 1)))[a]
        for t in range(2):
            rows = pl.ds(2 * t, 2)
            value = dot(full[j, rows].reshape(256, 512), near[c], dims) + dot(
                other[j, rows].reshape(256, 512), far[...], dims
            )
            if i == 0:
                reduce.so[t] = value.astype(BF)
            elif i == 1 and t == 0:
                reduce.kr[0] = value
            elif i == 1:
                reduce.sr[1] = value.astype(BF)
            elif i == 2 and t == 0:
                reduce.sl[0] = value.astype(BF)
            elif i == 2:
                reduce.kl[0] = value
            else:
                reduce.own[t] = value
        if i == 0:
            reduce.opposite()
        if i == 2:
            reduce.direct()

    zred = [Reduce(links, zb.at[a], zk.at[a], zw.at[a], zring) for a in range(2)]
    local[0].wait()
    begin(0, 0)
    begin(0, 1)
    local[1].wait()
    begin(0, 2)
    begin(1, 0)
    for copy in local[2:]:
        copy.wait()
    w_swap = (links.push(win.at[1 - c], wino, core), links.push(wout.at[1 - c], wouto, core))
    widen(0, 0)
    widen(0, 1)
    widen(0, 2)
    begin(1, 1), begin(1, 2), begin(0, 3), begin(1, 3)
    links.recv(w_swap[0], wino)
    links.recv(w_swap[1], wouto)
    widen(1, 0)
    widen_finish(0, 0)
    project(0, 0, zred[0])
    widen_finish(0, 1)
    widen_finish(0, 2)
    project(0, 1, zred[0])
    project(0, 2, zred[0])
    widen(1, 1), widen(1, 2), widen(0, 3), widen(1, 3)
    widen_finish(1, 0)
    project(1, 0, zred[1])
    zred[0].combine()
    widen_finish(1, 1)
    project(1, 1, zred[1])
    widen_finish(1, 2)
    project(1, 2, zred[1])
    widen_finish(0, 3)
    project(0, 3, zred[0])
    widen_finish(1, 3)
    project(1, 3, zred[1])
    zred[1].combine()

    hidden = [
        Gather(links, lambda p: Act.at[c, p], zring, Act.at[c, pl.ds(0, 3)]),
        Gather(links, lambda p: Pg.at[c, p], zring, Pg.at[c, pl.ds(0, 3)]),
    ]
    spread, spread_send = [{}, {}], [links.sends(full.at[c]) for full in (Act, Pg)]

    def spread_to(a, j, b):
        full = (Act, Pg)[a]
        spread[a][b] = links.push(full.at[c, j], full.at[c, j], core, spread_send[a])

    blocks = (k, wrap(k + 3), wrap(k + 1), wrap(k + 2))

    zred[0].arrive()
    for hh in range(2):

        @pl.loop(0, 8)
        def _(r):
            rows = pl.ds(pl.multiple_of(r * 32, 32), 32)
            act, gain = gelu_parts(zred[0].total(hh, rows))
            Act[c, k, hh, rows] = act.astype(BF)
            slope[hh, rows] = gain

    spread_to(0, k, 0)
    hidden[0].start()
    zred[1].arrive()
    for hh in range(2):

        @pl.loop(0, 8)
        def _(r):
            rows = pl.ds(pl.multiple_of(r * 32, 32), 32)
            Pg[c, k, hh, rows] = (zred[1].total(hh, rows) * slope[hh, rows]).astype(BF)

    spread_to(1, k, 0)
    hidden[1].start()

    plane = {}

    def parts(a, b):
        if a + b == 4:
            return [(7, 0, slice(0, 256)), (8, 1, slice(256, 512))]
        return [(4 * a + b, (a + b) % 2, slice(0, 512))]

    def emit(a, b):
        j = blocks[b]
        full = (Act, Pg)[a]
        links.recv(spread[a][b], full.at[1 - c, j])
        for t in range(2):
            if a == 0:
                value = dot(Act[0, j, t], wout[0], (1, 0)) + dot(Act[1, j, t], wout[1], (1, 0))
            else:
                value = dot(Pg[0, j, t], win[0], (1, 1)) + dot(Pg[1, j, t], win[1], (1, 1))
            O[pl.ds(2 * t, 2)] = value.reshape(2, 4, 2, 16, 512)
        for n, turn, cols in parts(a, b):
            plane[n] = one = (ydirect, xdirect)[turn](False)
            send, recv = links.sends(b1.at[n, pl.ds(0, 3), :, :, :, cols]), links.recvs()
            for r in (2, 1, 3):
                p = wrap(one.p + r)
                piece = O[p, :, :, :, cols] if turn == 0 else O[:, p, :, :, cols]
                src, dst = [b1.at[n, s, :, :, :, cols] for s in (r - 1, r + 2)]
                src[...] = piece.astype(BF)
                one.push((r, 0), src, dst, send, recv)
        for n, turn, cols in parts(a, b):
            p = plane[n].p
            w1[n, :, :, :, cols] = O[p, :, :, :, cols] if turn == 0 else O[:, p, :, :, cols]

    def narrow(a, b):
        for n, turn, cols in parts(a, b):
            one = plane[n]
            value = w1[n, :, :, :, cols]
            one.recv((2, 0), b1.at[n, pl.ds(3, 3), :, :, :, cols])
            for r in (1, 3, 2):
                value = value + b1[n, 2 + r, :, :, :, cols].astype(F32)
            O[0, :, :, :, cols] = value
            last = a + b == 4
            plane[n] = two = (xdirect, ydirect)[turn](last)
            send, recv = links.sends(b2.at[n, pl.ds(0, 7), 0, :, cols] if last else b2.at[n, pl.ds(0, 3)]), links.recvs()
            for r, dd in sorted(two.to, key=lambda key: (key[0] != 2, key)):
                p = wrap(two.p + r)
                if last:
                    s = 2 * r + dd - 1
                    src, dst = [b2.at[n, t, 0, :, cols] for t in (s, 7 + s)]
                    src[...] = O[0, p, d if dd == 0 else 1 - d, :, cols].astype(BF)
                else:
                    src, dst = b2.at[n, r - 1], b2.at[n, 2 + r]
                    src[...] = O[0, p].astype(BF)
                two.push((r, dd), src, dst, send, recv)
            w2[n, :, :, cols] = O[0, two.p, :, :, cols]

    def pair(a, b):
        ((n, turn, cols),) = parts(a, b)
        two = plane[n]
        value = w2[n]
        two.recv((2, 0), b2.at[n, pl.ds(3, 3)])
        for r in (1, 3, 2):
            value = value + b2[n, 2 + r].astype(F32)
        w2[n] = value
        b2[n, 6, 0] = w2[n, 1 - d].astype(BF)
        plane[n] = links.push(b2.at[n, 6, 0], b2.at[n, 7, 0], {"dp": 1 - d})

    def close(a, b):
        for n, turn, cols in parts(a, b):
            value = w2[n, d, :, cols]
            if a + b == 4:
                plane[n].recv((2, 1), b2.at[n, pl.ds(7, 7), 0, :, cols])
                for t in range(7, 14):
                    value = value + b2[n, t, 0, :, cols].astype(F32)
            else:
                links.recv(plane[n], b2.at[n, 7, 0])
                value = value + b2[n, 7, 0].astype(F32)
            (out_o, gx_o)[a][blocks[b], :, cols] = value.astype(BF)

    def weights(a, b):
        j = blocks[b]
        for h in range(2):
            value = None
            for t in range(2):
                rows = pl.ds(2 * t, 2)
                if a == 0:
                    term = dot(Act[h, j, t], G[j, rows].reshape(256, 512), (0, 0))
                else:
                    term = dot(X[j, rows].reshape(256, 512), Pg[h, j, t], (0, 0))
                value = term if value is None else value + term
            acc = (acco, acci)[a]
            if b > 0:
                value = value + acc[h]
            if b < 3:
                acc[h] = value
            elif a == 0:
                gwo_o[h] = value.astype(BF)
            else:
                gwi_o[:, h * 256 : (h + 1) * 256] = value.astype(BF)

    def relay(a):
        hidden[a].relay()
        spread_to(a, blocks[1], 1)
        spread_to(a, blocks[2], 2)

    def finish(a):
        hidden[a].finish()
        spread_to(a, blocks[3], 3)

    emit(0, 0)
    emit(1, 0)
    weights(0, 0)
    weights(1, 0)
    relay(0)
    emit(0, 1)
    emit(0, 2)
    narrow(0, 0)
    narrow(1, 0)
    weights(0, 1)
    weights(0, 2)
    pair(0, 0)
    pair(1, 0)
    relay(1)
    emit(1, 1)
    emit(1, 2)
    narrow(0, 1)
    narrow(0, 2)
    weights(1, 1)
    weights(1, 2)
    finish(0)
    emit(0, 3)
    weights(0, 3)
    pair(0, 1)
    pair(0, 2)
    finish(1)
    emit(1, 3)
    narrow(1, 1)
    narrow(1, 2)
    weights(1, 3)
    narrow(0, 3)
    pair(1, 1)
    pair(1, 2)
    close(0, 0), close(1, 0), close(0, 1), close(0, 2)
    narrow(1, 3)
    pair(0, 3)
    close(1, 1), close(1, 2), close(0, 3)
    close(1, 3)
    links.drain()
    assert (len(links.sent), links.got) == (SENDS, RECVS), (len(links.sent), links.got)


def store(*refs):
    copies = [pltpu.make_async_copy(refs[i], refs[4 + i], refs[8].at[i]) for i in range(4)]
    for copy in copies:
        copy.start()
    for copy in copies:
        copy.wait()


def on_device(tokens, w_in, w_out, out_grad):
    any_spec = pl.BlockSpec(memory_space=pl.ANY)
    vmem = pl.BlockSpec(memory_space=pltpu.VMEM)
    full = pltpu.VMEM((4, 4, 4, 2, 16, 512), BF)
    hid = pltpu.VMEM((2, 4, 2, 256, 256), BF)
    results = pl.pallas_call(
        kernel,
        out_shape=(
            pltpu.VMEM((4, 16, 512), BF),
            pltpu.VMEM((4, 16, 512), BF),
            pltpu.VMEM((512, 512), BF),
            pltpu.VMEM((2, 256, 512), BF),
        ),
        in_specs=[any_spec] * 4,
        out_specs=(vmem,) * 4,
        scratch_shapes=[
            full, full, full, full,
            pltpu.VMEM((2, 512, 256), BF),
            pltpu.VMEM((512, 256), BF),
            pltpu.VMEM((2, 256, 512), BF),
            pltpu.VMEM((256, 512), BF),
            hid, hid,
            pltpu.VMEM((2, 6, 2, 256, 256), BF),
            pltpu.VMEM((2, 2, 1, 256, 256), F32),
            pltpu.VMEM((2, 2, 256, 256), F32),
            pltpu.VMEM((2, 256, 256), F32),
            pltpu.VMEM((4, 4, 2, 16, 512), F32),
            pltpu.VMEM((9, 6, 4, 2, 16, 512), BF),
            pltpu.VMEM((9, 4, 2, 16, 512), F32),
            pltpu.VMEM((9, 14, 2, 16, 512), BF),
            pltpu.VMEM((9, 2, 16, 512), F32),
            pltpu.VMEM((2, 256, 512), F32),
            pltpu.VMEM((2, 512, 256), F32),
            pltpu.SemaphoreType.DMA((5,)),
            pltpu.SemaphoreType.DMA((SENDS,)),
            pltpu.SemaphoreType.DMA((RECVS,)),
        ],
        compiler_params=pltpu.CompilerParams(
            collective_id=0, has_side_effects=True, vmem_limit_bytes=58 << 20
        ),
        name="ffn",
    )(
        tokens.reshape(4, 16, 512),
        w_in,
        w_out.reshape(2, 2, 256, 512),
        out_grad.reshape(4, 16, 512),
    )
    results = [pltpu.with_memory_space_constraint(r, pltpu.VMEM) for r in results]
    output, grad_x, gw_in, gw_out = pl.pallas_call(
        store,
        out_shape=tuple(jax.ShapeDtypeStruct(r.shape, BF) for r in results),
        in_specs=[vmem] * 4,
        out_specs=(any_spec,) * 4,
        scratch_shapes=[pltpu.SemaphoreType.DMA((4,))],
        name="store",
    )(*results)
    return (
        output.reshape(64, 512),
        grad_x.reshape(64, 512),
        gw_in.reshape(512, 1, 512),
        gw_out.reshape(1, 512, 512),
    )


def solution(mesh):
    placed = (P(("dp", "col"), "row"), P("row", "col"), P("col", "row"), P(("dp", "col"), "row"))
    return jax.shard_map(
        on_device,
        mesh=mesh,
        in_specs=placed,
        out_specs=(
            P(("dp", "col"), "row"),
            P(("dp", "col"), "row"),
            P("row", "col", "dp"),
            P("col", "dp", "row"),
        ),
        check_vma=False,
    )
```

```python
import math

import jax
import jax.numpy as jnp
from jax import lax
from jax.experimental import pallas as pl
from jax.experimental.pallas import tpu as pltpu
from jax.sharding import PartitionSpec as P

F32, BF = jnp.float32, jnp.bfloat16
MESH = pl.DeviceIdType.MESH
SENDS, RECVS = 64, 118


def gelu_parts(pre):
    cdf = 0.5 * (1.0 + lax.erf(pre * (1.0 / math.sqrt(2.0))))
    pdf = jnp.exp(-0.5 * pre * pre) * (1.0 / math.sqrt(2.0 * math.pi))
    return pre * cdf, cdf + pre * pdf


def dot(left, right, dims):
    return lax.dot_general(left, right, ((dims[:1], dims[1:]), ((), ())), preferred_element_type=F32)


def wrap(p):
    return lax.rem(p, 4)


class Links:
    def __init__(self, ssem, rsem):
        self.ssem, self.rsem, self.sent, self.got, self.dev = ssem, rsem, [], 0, None

    def make(self, send, recv, src, dst, dev):
        return pltpu.make_async_remote_copy(
            src_ref=src,
            dst_ref=dst,
            send_sem=self.ssem.at[send],
            recv_sem=self.rsem.at[recv],
            device_id=dev,
            device_id_type=MESH,
        )

    def sends(self, total):
        self.sent.append(total)
        return len(self.sent) - 1

    def recvs(self):
        self.got += 1
        return self.got - 1

    def push(self, src, dst, dev, send=None, recv=None):
        send = self.sends(src) if send is None else send
        recv = self.recvs() if recv is None else recv
        self.make(send, recv, src, dst, dev).start()
        self.dev = dev
        return recv

    def recv(self, n, ref):
        self.make(0, n, ref, ref, self.dev).wait_recv()

    def drain(self):
        for n, total in enumerate(self.sent):
            self.make(n, 0, total, total, self.dev).wait_send()


def part(ref, half):
    n = ref.shape[0] // 2
    return ref.at[pl.ds(half * n, n)]


class Gather:
    def __init__(self, links, slot, ring, total):
        self.links, self.slot, (self.p, self.left, self.right) = links, slot, ring
        self.send, self.c = links.sends(total), links.recvs()

    def start(self):
        mine = self.slot(self.p)
        self.a = self.links.push(mine, mine, self.right, self.send)
        self.b = self.links.push(mine, mine, self.left, self.send)

    def relay(self):
        near = self.slot(wrap(self.p + 3))
        self.links.recv(self.a, near)
        near = part(near, 0)
        self.links.push(near, near, self.right, self.send, self.c)
        near = self.slot(wrap(self.p + 1))
        self.links.recv(self.b, near)
        near = part(near, 1)
        self.links.push(near, near, self.left, self.send, self.c)

    def finish(self):
        self.links.recv(self.c, self.slot(wrap(self.p + 2)))


class Direct:
    def __init__(self, links, ring, col, dp, twins):
        self.links, self.p, self.sent = links, ring, {}
        self.to = {}
        for r in range(4):
            for dd in range(2 if twins else 1):
                if r + dd > 0:
                    dev = {"col": col(wrap(ring + r))}
                    if dd == 1:
                        dev = {"dp": 1 - dp} if r == 0 else {**dev, "dp": 1 - dp}
                    self.to[r, dd] = dev

    def push(self, key, src, dst, send, recv=None):
        self.sent[key] = self.links.push(src, dst, self.to[key], send, recv)

    def recv(self, key, ref):
        self.links.recv(self.sent[key], ref)


class Reduce:
    def __init__(self, links, bufs, keep, own, ring):
        self.links, (self.p, self.left, self.right) = links, ring
        self.so, self.sr, self.sl, self.ro, self.rl, self.rr = [bufs.at[i] for i in range(6)]
        self.kr, self.kl, self.own, self.both = keep.at[0], keep.at[1], own, bufs.at[pl.ds(4, 2)]
        self.send = links.sends(bufs.at[pl.ds(0, 3)])
        self.a, self.b, self.c = links.recvs(), links.recvs(), links.recvs()

    def put(self, i, at, value):
        push, half = self.links.push, [(*at, slice(None), h) if len(at) == 1 else (*at, h) for h in range(2)]
        if i == 0:
            self.so[at] = value.astype(BF)
            push(self.so.at[half[0]], self.ro.at[half[0]], self.right, self.send, self.a)
            push(self.so.at[half[1]], self.ro.at[half[1]], self.left, self.send, self.b)
        elif i == 1:
            self.sr[half[1]] = value[:, 1].astype(BF)
            push(self.sr.at[half[1]], self.rl.at[half[1]], self.right, self.send, self.c)
            self.kr[at] = value[:, 0]
        elif i == 2:
            self.sl[half[0]] = value[:, 0].astype(BF)
            push(self.sl.at[half[0]], self.rr.at[half[0]], self.left, self.send, self.c)
            self.kl[at] = value[:, 1]
        else:
            self.own[at] = value

    def combine(self):
        ways = (
            (self.a, self.sr, self.kr, self.rl, self.right),
            (self.b, self.sl, self.kl, self.rr, self.left),
        )
        for h, (sem, send, keep, to, dev) in enumerate(ways):
            self.links.recv(sem, self.ro.at[:, :, h])
            send[:, :, h] = (keep[...] + self.ro[:, :, h].astype(F32)).astype(BF)
            self.links.push(send.at[:, :, h], to.at[:, :, h], dev, self.send, self.c)

    def arrive(self):
        self.links.recv(self.c, self.both)

    def total(self, *at):
        return self.own[at] + self.rl[at].astype(F32) + self.rr[at].astype(F32)


def kernel(
    tok, w_in, w_out, og,
    out_o, gx_o, gwi_o, gwo_o,
    X, XO, G, GO, win, wino, wout, wouto,
    Act, Pg, zb, zk, zw, slope,
    O, b1, w1, b2, w2, acco, acci,
    lsem, ssem, rsem,
):
    d, row, col = lax.axis_index("dp"), lax.axis_index("row"), lax.axis_index("col")
    k, c = lax.div(row, 2), lax.rem(row, 2)
    y, x = lax.div(col, 4), lax.rem(col, 4)
    core = {"row": 2 * k + (1 - c)}
    zring = (k, {"row": 2 * wrap(k + 3) + c}, {"row": 2 * wrap(k + 1) + c})
    links = Links(ssem, rsem)

    def xdirect(twins):
        return Direct(links, x, lambda p: 4 * y + p, d, twins)

    def ydirect(twins):
        return Direct(links, y, lambda p: 4 * p + x, d, twins)

    local = [
        pltpu.make_async_copy(tok, X.at[:, y, x, d], lsem.at[0]),
        pltpu.make_async_copy(og, G.at[:, y, x, d], lsem.at[1]),
        pltpu.make_async_copy(w_out.at[d], wout, lsem.at[2]),
        pltpu.make_async_copy(w_in.at[:, pl.ds(pl.multiple_of(d * 512, 512), 256)], win.at[0], lsem.at[3]),
        pltpu.make_async_copy(w_in.at[:, pl.ds(pl.multiple_of(d * 512 + 256, 256), 256)], win.at[1], lsem.at[4]),
    ]
    for copy in local:
        copy.start()
    barrier = pltpu.get_barrier_semaphore()
    peers = [core, zring[1], zring[2], *xdirect(True).to.values()]
    peers += [dev for (r, _), dev in ydirect(True).to.items() if r > 0]
    for dev in peers:
        pl.semaphore_signal(barrier, inc=1, device_id=dev, device_id_type=MESH)
    pl.semaphore_wait(barrier, len(peers))

    js = (wrap(k + 2), wrap(k + 1), wrap(k + 3), k)
    first, second, shares = {}, {}, {}

    def turn(a, i):
        return (a + i) % 2

    def slab(a, i, full, p):
        return (full.at[js[i], p], full.at[js[i], :, p])[turn(a, i)]

    def begin(a, i):
        both = a == 0 and i < 2
        first[a, i] = one = (xdirect, ydirect)[turn(a, i)](both)
        j, recv = js[i], links.recvs()
        if both:
            mine, send = (X, G)[a].at[j, y, x, d], links.sends(b2.at[8, pl.ds(0, 7), 0])
        else:
            links.recv(twins[a, i], (X, G)[a].at[j, y, x, 1 - d])
            mine, send = (X, G)[a].at[j, y, x], links.sends(b2.at[8, pl.ds(0, 3)])
        for key in sorted(one.to, key=lambda key: (key[0] == 2, key)):
            one.push(key, mine, mine, send, recv)

    def share(a, i, q):
        two = second[a, i]
        p = wrap(two.p + (0, 3, 1, 2)[q])
        if q == 0:
            shares[a, i] = links.sends((X, G)[a].at[js[i]])
        full, other = ((X, XO), (G, GO))[a]
        shares[a, i, q] = (p, links.push(slab(a, i, full, p), slab(a, i, other, p), core, shares[a, i]))

    def widen(a, i):
        full = (X, G)[a]
        both = a == 0 and i < 2
        first[a, i].recv((2, 0), b2.at[8, pl.ds(0, 7), 0] if both else b2.at[8, pl.ds(0, 3)])
        second[a, i] = two = (ydirect, xdirect)[turn(a, i)](False)
        share(a, i, 0)
        mine, two.send = slab(a, i, full, two.p), links.sends(full.at[js[i], pl.ds(0, 3)])
        for r in (1, 3):
            two.push((r, 0), mine, mine, two.send)
        two.sent[2, 0] = links.recvs()

    def fetch(a, i, q):
        two = second[a, i]
        r = (0, 1, 3, 2)[q]
        ref = slab(a, i, (X, G)[a], wrap(two.p + 4 - r))
        two.recv((r, 0), ref)
        if q < 3:
            half = part(ref, q - 1)
            links.push(half, half, two.to[r, 0], two.send, two.sent[2, 0])
        share(a, i, q)

    def project(a, i, q):
        p, sem = shares[a, i, q]
        full, other, near, far, dims = ((X, XO, win, wino, (1, 0)), (G, GO, wout, wouto, (1, 1)))[a]
        links.recv(sem, slab(a, i, other, p))
        value = dot(slab(a, i, full, p)[...].reshape(128, 512), near[c], dims) + dot(
            slab(a, i, other, p)[...].reshape(128, 512), far[...], dims
        )
        at = (p,) if turn(a, i) == 0 else (slice(None), p)
        zred[a].put(i, at, value.reshape(4, 2, 16, 256))

    zred = [Reduce(links, zb.at[a], zk.at[a], zw.at[a], zring) for a in range(2)]
    def run(steps):
        act = {"B": begin, "W": widen, "F": fetch, "P": project}
        for step in steps.split():
            act[step[0]](*[int(v) for v in step[1:]])

    local[0].wait()
    run("B00 B01")
    twins = {}
    for a, i in ((0, 2), (1, 0), (1, 1), (1, 2), (0, 3), (1, 3)):
        if (a, i) == (1, 0):
            local[1].wait()
        mine = (X, G)[a].at[js[i], y, x, d]
        twins[a, i] = links.push(mine, mine, {"dp": 1 - d})
    for copy in local[2:]:
        copy.wait()
    w_swap = (links.push(win.at[1 - c], wino, core), links.push(wout.at[1 - c], wouto, core))
    run("B02 B10 W00 W01")
    links.recv(w_swap[0], wino)
    links.recv(w_swap[1], wouto)
    run("P000 P010 W02 W10 B11 B12 P020 P100")
    run("F001 F002 F011 F012 P001 P002 P011 P012")
    run("F021 F022 F003 P021 P022 F013 P003 P013")
    run("F101 F102 F023 W11 W12 B03 B13 P101 P102 P023 F103 P110 P120 P103")
    zred[0].combine()
    run("F111 F112 F121 F122 P111 P112 P121 P122 F113 F123 W03 W13 P113 P123")
    zred[1].combine()
    run("F031 F032 F131 F132 P030 P031 P032 F033 P033 F133")

    hidden = [
        Gather(links, lambda p: Act.at[c, p], zring, Act.at[c, pl.ds(0, 3)]),
        Gather(links, lambda p: Pg.at[c, p], zring, Pg.at[c, pl.ds(0, 3)]),
    ]
    spread, spread_send = [{}, {}], [links.sends(full.at[c]) for full in (Act, Pg)]

    def spread_to(a, j, b):
        full = (Act, Pg)[a]
        spread[a][b] = links.push(full.at[c, j], full.at[c, j], core, spread_send[a])

    blocks = (k, wrap(k + 3), wrap(k + 1), wrap(k + 2))

    zred[0].arrive()

    @pl.loop(0, 16)
    def _(r):
        at = (lax.div(r, 4), lax.rem(r, 4))
        act, gain = gelu_parts(zred[0].total(*at))
        Act[(c, k, *at)] = act.astype(BF)
        slope[at] = gain

    spread_to(0, k, 0)
    hidden[0].start()
    run("P130 P131 P132 P133")
    zred[1].arrive()

    @pl.loop(0, 16)
    def _(r):
        at = (lax.div(r, 4), lax.rem(r, 4))
        Pg[(c, k, *at)] = (zred[1].total(*at) * slope[at]).astype(BF)

    spread_to(1, k, 0)
    hidden[1].start()

    plane = {}

    def parts(a, b):
        if b == 3:
            return [(3 + 4 * a, 0, slice(0, 256)), (8 + a, 1, slice(256, 512))]
        return [(4 * a + b, (a + b) % 2, slice(0, 512))]

    def emit(a, b):
        j = blocks[b]
        full = (Act, Pg)[a]
        links.recv(spread[a][b], full.at[1 - c, j])
        for t in range(2):
            rows = pl.ds(2 * t, 2)
            left = [full[h, j, rows].reshape(256, 256) for h in range(2)]
            if a == 0:
                value = dot(left[0], wout[0], (1, 0)) + dot(left[1], wout[1], (1, 0))
            else:
                value = dot(left[0], win[0], (1, 1)) + dot(left[1], win[1], (1, 1))
            O[rows] = value.reshape(2, 4, 2, 16, 512)
        for n, turn, cols in parts(a, b):
            plane[n] = one = (ydirect, xdirect)[turn](False)
            send, recv = links.sends(b1.at[n, pl.ds(0, 3), :, :, :, cols]), links.recvs()
            for r in (2, 1, 3):
                p = wrap(one.p + r)
                piece = O[p, :, :, :, cols] if turn == 0 else O[:, p, :, :, cols]
                src, dst = [b1.at[n, s, :, :, :, cols] for s in (r - 1, r + 2)]
                src[...] = piece.astype(BF)
                one.push((r, 0), src, dst, send, recv)
        for n, turn, cols in parts(a, b):
            p = plane[n].p
            w1[n, :, :, :, cols] = O[p, :, :, :, cols] if turn == 0 else O[:, p, :, :, cols]

    def narrow(a, b):
        for n, turn, cols in parts(a, b):
            one = plane[n]
            value = w1[n, :, :, :, cols]
            one.recv((2, 0), b1.at[n, pl.ds(3, 3), :, :, :, cols])
            for r in (1, 3, 2):
                value = value + b1[n, 2 + r, :, :, :, cols].astype(F32)
            O[0, :, :, :, cols] = value
            last = b == 3
            plane[n] = two = (xdirect, ydirect)[turn](last)
            send, recv = links.sends(b2.at[n, pl.ds(0, 7), 0, :, cols] if last else b2.at[n, pl.ds(0, 3)]), links.recvs()
            for r, dd in sorted(two.to, key=lambda key: (key[0] != 2, key)):
                p = wrap(two.p + r)
                if last:
                    s = 2 * r + dd - 1
                    src, dst = [b2.at[n, t, 0, :, cols] for t in (s, 7 + s)]
                    src[...] = O[0, p, d if dd == 0 else 1 - d, :, cols].astype(BF)
                else:
                    src, dst = b2.at[n, r - 1], b2.at[n, 2 + r]
                    src[...] = O[0, p].astype(BF)
                two.push((r, dd), src, dst, send, recv)
            w2[n, :, :, cols] = O[0, two.p, :, :, cols]

    def pair(a, b):
        ((n, turn, cols),) = parts(a, b)
        two = plane[n]
        value = w2[n]
        two.recv((2, 0), b2.at[n, pl.ds(3, 3)])
        for r in (1, 3, 2):
            value = value + b2[n, 2 + r].astype(F32)
        w2[n] = value
        b2[n, 6, 0] = w2[n, 1 - d].astype(BF)
        plane[n] = links.push(b2.at[n, 6, 0], b2.at[n, 7, 0], {"dp": 1 - d})

    def close(a, b):
        for n, turn, cols in parts(a, b):
            value = w2[n, d, :, cols]
            if b == 3:
                plane[n].recv((2, 1), b2.at[n, pl.ds(7, 7), 0, :, cols])
                for t in range(7, 14):
                    value = value + b2[n, t, 0, :, cols].astype(F32)
            else:
                links.recv(plane[n], b2.at[n, 7, 0])
                value = value + b2[n, 7, 0].astype(F32)
            (out_o, gx_o)[a][blocks[b], :, cols] = value.astype(BF)

    def weights(a, b):
        j = blocks[b]
        for h in range(2):
            value = None
            for t in range(2):
                rows = pl.ds(2 * t, 2)
                hid = (Act, Pg)[a][h, j, rows].reshape(256, 256)
                wide = (G, X)[a][j, rows].reshape(256, 512)
                term = dot(hid, wide, (0, 0)) if a == 0 else dot(wide, hid, (0, 0))
                value = term if value is None else value + term
            acc = (acco, acci)[a]
            if b > 0:
                value = value + acc[h]
            if b < 3:
                acc[h] = value
            elif a == 0:
                gwo_o[h] = value.astype(BF)
            else:
                gwi_o[:, h * 256 : (h + 1) * 256] = value.astype(BF)

    def relay(a):
        hidden[a].relay()
        spread_to(a, blocks[1], 1)
        spread_to(a, blocks[2], 2)

    def finish(a):
        hidden[a].finish()
        spread_to(a, blocks[3], 3)

    emit(0, 0)
    emit(1, 0)
    weights(0, 0)
    weights(1, 0)
    relay(0)
    emit(0, 1)
    emit(0, 2)
    narrow(0, 0)
    narrow(1, 0)
    weights(0, 1)
    weights(0, 2)
    relay(1)
    emit(1, 1)
    emit(1, 2)
    pair(0, 0)
    pair(1, 0)
    narrow(0, 1)
    narrow(0, 2)
    weights(1, 1)
    weights(1, 2)
    finish(0)
    emit(0, 3)
    weights(0, 3)
    finish(1)
    emit(1, 3)
    narrow(1, 1)
    narrow(1, 2)
    pair(0, 1)
    pair(0, 2)
    weights(1, 3)
    narrow(0, 3)
    close(0, 0), close(1, 0), close(0, 1), close(0, 2)
    narrow(1, 3)
    pair(1, 1)
    pair(1, 2)
    close(1, 1), close(1, 2), close(0, 3)
    close(1, 3)
    links.drain()
    assert (len(links.sent), links.got) == (SENDS, RECVS), (len(links.sent), links.got)


def store(*refs):
    copies = [pltpu.make_async_copy(refs[i], refs[4 + i], refs[8].at[i]) for i in range(4)]
    for copy in copies:
        copy.start()
    for copy in copies:
        copy.wait()


def on_device(tokens, w_in, w_out, out_grad):
    any_spec = pl.BlockSpec(memory_space=pl.ANY)
    vmem = pl.BlockSpec(memory_space=pltpu.VMEM)
    full = pltpu.VMEM((4, 4, 4, 2, 16, 512), BF)
    hid = pltpu.VMEM((2, 4, 4, 4, 2, 16, 256), BF)
    results = pl.pallas_call(
        kernel,
        out_shape=(
            pltpu.VMEM((4, 16, 512), BF),
            pltpu.VMEM((4, 16, 512), BF),
            pltpu.VMEM((512, 512), BF),
            pltpu.VMEM((2, 256, 512), BF),
        ),
        in_specs=[any_spec] * 4,
        out_specs=(vmem,) * 4,
        scratch_shapes=[
            full, full, full, full,
            pltpu.VMEM((2, 512, 256), BF),
            pltpu.VMEM((512, 256), BF),
            pltpu.VMEM((2, 256, 512), BF),
            pltpu.VMEM((256, 512), BF),
            hid, hid,
            pltpu.VMEM((2, 6, 4, 4, 2, 16, 256), BF),
            pltpu.VMEM((2, 2, 4, 4, 16, 256), F32),
            pltpu.VMEM((2, 4, 4, 2, 16, 256), F32),
            pltpu.VMEM((4, 4, 2, 16, 256), F32),
            pltpu.VMEM((4, 4, 2, 16, 512), F32),
            pltpu.VMEM((10, 6, 4, 2, 16, 512), BF),
            pltpu.VMEM((10, 4, 2, 16, 512), F32),
            pltpu.VMEM((10, 14, 2, 16, 512), BF),
            pltpu.VMEM((10, 2, 16, 512), F32),
            pltpu.VMEM((2, 256, 512), F32),
            pltpu.VMEM((2, 512, 256), F32),
            pltpu.SemaphoreType.DMA((5,)),
            pltpu.SemaphoreType.DMA((SENDS,)),
            pltpu.SemaphoreType.DMA((RECVS,)),
        ],
        compiler_params=pltpu.CompilerParams(
            collective_id=0, has_side_effects=True, vmem_limit_bytes=58 << 20
        ),
        name="ffn",
    )(
        tokens.reshape(4, 16, 512),
        w_in,
        w_out.reshape(2, 2, 256, 512),
        out_grad.reshape(4, 16, 512),
    )
    results = [pltpu.with_memory_space_constraint(r, pltpu.VMEM) for r in results]
    output, grad_x, gw_in, gw_out = pl.pallas_call(
        store,
        out_shape=tuple(jax.ShapeDtypeStruct(r.shape, BF) for r in results),
        in_specs=[vmem] * 4,
        out_specs=(any_spec,) * 4,
        scratch_shapes=[pltpu.SemaphoreType.DMA((4,))],
        name="store",
    )(*results)
    return (
        output.reshape(64, 512),
        grad_x.reshape(64, 512),
        gw_in.reshape(512, 1, 512),
        gw_out.reshape(1, 512, 512),
    )


def solution(mesh):
    placed = (P(("dp", "col"), "row"), P("row", "col"), P("col", "row"), P(("dp", "col"), "row"))
    return jax.shard_map(
        on_device,
        mesh=mesh,
        in_specs=placed,
        out_specs=(
            P(("dp", "col"), "row"),
            P(("dp", "col"), "row"),
            P("row", "col", "dp"),
            P("col", "dp", "row"),
        ),
        check_vma=False,
    )
```

```python
import math

import jax
import jax.numpy as jnp
from jax import lax
from jax.experimental import pallas as pl
from jax.experimental.pallas import tpu as pltpu
from jax.sharding import PartitionSpec as P

F32, BF = jnp.float32, jnp.bfloat16
MESH = pl.DeviceIdType.MESH
SENDS, RECVS = 32, 130


def gelu_parts(pre):
    cdf = 0.5 * (1.0 + lax.erf(pre * (1.0 / math.sqrt(2.0))))
    pdf = jnp.exp(-0.5 * pre * pre) * (1.0 / math.sqrt(2.0 * math.pi))
    return pre * cdf, cdf + pre * pdf


def dot(left, right, dims):
    return lax.dot_general(left, right, ((dims[:1], dims[1:]), ((), ())), preferred_element_type=F32)


def wrap(p):
    return lax.rem(p, 4)


class Links:
    def __init__(self, ssem, rsem):
        self.ssem, self.rsem, self.sent, self.got, self.dev = ssem, rsem, [], 0, None

    def make(self, send, recv, src, dst, dev):
        return pltpu.make_async_remote_copy(
            src_ref=src,
            dst_ref=dst,
            send_sem=self.ssem.at[send],
            recv_sem=self.rsem.at[recv],
            device_id=dev,
            device_id_type=MESH,
        )

    def sends(self, total):
        self.sent.append(total)
        return len(self.sent) - 1

    def recvs(self):
        self.got += 1
        return self.got - 1

    def push(self, src, dst, dev, send=None, recv=None):
        send = self.sends(src) if send is None else send
        recv = self.recvs() if recv is None else recv
        self.make(send, recv, src, dst, dev).start()
        self.dev = dev
        return recv

    def recv(self, n, ref):
        self.make(0, n, ref, ref, self.dev).wait_recv()

    def drain(self):
        for n, total in enumerate(self.sent):
            self.make(n, 0, total, total, self.dev).wait_send()


def part(ref, half):
    n = ref.shape[0] // 2
    return ref.at[pl.ds(half * n, n)]


class Gather:
    def __init__(self, links, slot, ring, total):
        self.links, self.slot, (self.p, self.left, self.right) = links, slot, ring
        self.send, self.c, self.near = links.sends(total), links.recvs(), {}

    def start(self, second):
        mine = self.slot(self.p)
        near, far = mine.at[:, :, second], mine.at[:, :, 1 - second]
        self.near[second] = (
            self.links.push(near, near, self.right, self.send),
            self.links.push(far, far, self.left, self.send),
        )

    def take(self, second):
        left, right = [self.slot(wrap(self.p + n)).at[:, :, h] for n, h in ((3, second), (1, 1 - second))]
        self.links.recv(self.near[second][0], left)
        self.links.recv(self.near[second][1], right)
        return left, right

    def relay(self):
        left, right = self.take(0)
        self.links.push(left, left, self.right, self.send, self.c)
        self.links.push(right, right, self.left, self.send, self.c)

    def finish(self):
        self.links.recv(self.c, self.slot(wrap(self.p + 2)))


class Direct:
    def __init__(self, links, ring, col, dp, twins):
        self.links, self.p, self.sent = links, ring, {}
        self.to = {}
        for r in range(4):
            for dd in range(2 if twins else 1):
                if r + dd > 0:
                    dev = {"col": col(wrap(ring + r))}
                    if dd == 1:
                        dev = {"dp": 1 - dp} if r == 0 else {**dev, "dp": 1 - dp}
                    self.to[r, dd] = dev

    def push(self, key, src, dst, send, recv=None):
        self.sent[key] = self.links.push(src, dst, self.to[key], send, recv)

    def recv(self, key, ref):
        self.links.recv(self.sent[key], ref)


class Reduce:
    def __init__(self, links, bufs, keep, own, ring):
        self.links, (self.p, self.left, self.right) = links, ring
        self.so, self.sr, self.sl, self.ro, self.rl, self.rr = [bufs.at[i] for i in range(6)]
        self.kr, self.kl, self.own, self.both = keep.at[0], keep.at[1], own, bufs.at[pl.ds(4, 2)]
        self.send = links.sends(bufs.at[pl.ds(0, 3)])
        self.a, self.b, self.c = links.recvs(), links.recvs(), links.recvs()

    def put(self, i, at, value):
        push, half = self.links.push, [(*at, slice(None), h) if len(at) == 1 else (*at, h) for h in range(2)]
        if i == 0:
            self.so[at] = value.astype(BF)
            push(self.so.at[half[0]], self.ro.at[half[0]], self.right, self.send, self.a)
            push(self.so.at[half[1]], self.ro.at[half[1]], self.left, self.send, self.b)
        elif i == 1:
            self.sr[half[1]] = value[:, 1].astype(BF)
            push(self.sr.at[half[1]], self.rl.at[half[1]], self.right, self.send, self.c)
            self.kr[at] = value[:, 0]
        elif i == 2:
            self.sl[half[0]] = value[:, 0].astype(BF)
            push(self.sl.at[half[0]], self.rr.at[half[0]], self.left, self.send, self.c)
            self.kl[at] = value[:, 1]
        else:
            self.own[at] = value

    def combine(self):
        ways = (
            (self.a, self.sr, self.kr, self.rl, self.right),
            (self.b, self.sl, self.kl, self.rr, self.left),
        )
        for h, (sem, send, keep, to, dev) in enumerate(ways):
            self.links.recv(sem, self.ro.at[:, :, h])
            send[:, :, h] = (keep[...] + self.ro[:, :, h].astype(F32)).astype(BF)
            self.links.push(send.at[:, :, h], to.at[:, :, h], dev, self.send, self.c)

    def arrive(self):
        self.links.recv(self.c, self.both)

    def total(self, *at):
        return self.own[at] + self.rl[at].astype(F32) + self.rr[at].astype(F32)


def kernel(
    tok, w_in, w_out, og,
    out_o, gx_o, gwi_o, gwo_o,
    X, XO, G, GO, win, wino, wout, wouto,
    Act, Pg, zb, zk, zw, slope,
    O, b1, w1, b2, w2, acco, acci,
    lsem, ssem, rsem,
):
    d, row, col = lax.axis_index("dp"), lax.axis_index("row"), lax.axis_index("col")
    k, c = lax.div(row, 2), lax.rem(row, 2)
    y, x = lax.div(col, 4), lax.rem(col, 4)
    core = {"row": 2 * k + (1 - c)}
    zring = (k, {"row": 2 * wrap(k + 3) + c}, {"row": 2 * wrap(k + 1) + c})
    links = Links(ssem, rsem)

    def xdirect(twins):
        return Direct(links, x, lambda p: 4 * y + p, d, twins)

    def ydirect(twins):
        return Direct(links, y, lambda p: 4 * p + x, d, twins)

    local = [
        pltpu.make_async_copy(tok, X.at[:, y, x, d], lsem.at[0]),
        pltpu.make_async_copy(og, G.at[:, y, x, d], lsem.at[1]),
        pltpu.make_async_copy(w_out.at[d], wout, lsem.at[2]),
        pltpu.make_async_copy(w_in.at[:, pl.ds(pl.multiple_of(d * 512, 512), 256)], win.at[0], lsem.at[3]),
        pltpu.make_async_copy(w_in.at[:, pl.ds(pl.multiple_of(d * 512 + 256, 256), 256)], win.at[1], lsem.at[4]),
    ]
    for copy in local:
        copy.start()
    barrier = pltpu.get_barrier_semaphore()
    peers = [core, zring[1], zring[2], *xdirect(True).to.values()]
    peers += [dev for (r, _), dev in ydirect(True).to.items() if r > 0]
    for dev in peers:
        pl.semaphore_signal(barrier, inc=1, device_id=dev, device_id_type=MESH)
    pl.semaphore_wait(barrier, len(peers))

    js = (wrap(k + 2), wrap(k + 1), wrap(k + 3), k)
    first, second, shares = {}, {}, {}
    share_send = [links.sends(full) for full in (X, G)]
    ring_send = [links.sends(full.at[:, pl.ds(0, 3)]) for full in (X, G)]
    first_send = [links.sends(b2.at[pl.ds(0, 2), pl.ds(0, 7), 0]), links.sends(b2.at[pl.ds(0, 6), pl.ds(0, 3)])]
    twin_send = links.sends(b2.at[pl.ds(0, 6), 0, 0])

    def turn(a, i):
        return (a + i) % 2

    def slab(a, i, full, p):
        return (full.at[js[i], p], full.at[js[i], :, p])[turn(a, i)]

    def begin(a, i):
        both = a == 0 and i < 2
        first[a, i] = one = (xdirect, ydirect)[turn(a, i)](both)
        j, recv = js[i], links.recvs()
        if both:
            mine, send = (X, G)[a].at[j, y, x, d], first_send[0]
        else:
            links.recv(twins[a, i], (X, G)[a].at[j, y, x, 1 - d])
            mine, send = (X, G)[a].at[j, y, x], first_send[1]
        for key in sorted(one.to, key=lambda key: (key[0] == 2, key)):
            one.push(key, mine, mine, send, recv)

    def share(a, i, q):
        two = second[a, i]
        p = wrap(two.p + (0, 3, 1, 2)[q])
        full, other = ((X, XO), (G, GO))[a]
        shares[a, i, q] = (p, links.push(slab(a, i, full, p), slab(a, i, other, p), core, share_send[a]))

    def widen(a, i):
        full = (X, G)[a]
        both = a == 0 and i < 2
        first[a, i].recv((2, 0), b2.at[8, pl.ds(0, 7), 0] if both else b2.at[8, pl.ds(0, 3)])
        second[a, i] = two = (ydirect, xdirect)[turn(a, i)](False)
        share(a, i, 0)
        mine, two.send = slab(a, i, full, two.p), ring_send[a]
        for r in (1, 3):
            two.push((r, 0), mine, mine, two.send)
        two.sent[2, 0] = links.recvs()

    def fetch(a, i, q):
        two = second[a, i]
        r = (0, 1, 3, 2)[q]
        ref = slab(a, i, (X, G)[a], wrap(two.p + 4 - r))
        two.recv((r, 0), ref)
        if q < 3:
            half = part(ref, q - 1)
            links.push(half, half, two.to[r, 0], two.send, two.sent[2, 0])
        share(a, i, q)

    def project(a, i, q):
        p, sem = shares[a, i, q]
        full, other, near, far, dims = ((X, XO, win, wino, (1, 0)), (G, GO, wout, wouto, (1, 1)))[a]
        links.recv(sem, slab(a, i, other, p))
        value = dot(slab(a, i, full, p)[...].reshape(128, 512), near[c], dims) + dot(
            slab(a, i, other, p)[...].reshape(128, 512), far[...], dims
        )
        at = (p,) if turn(a, i) == 0 else (slice(None), p)
        zred[a].put(i, at, value.reshape(4, 2, 16, 256))

    zred = [Reduce(links, zb.at[a], zk.at[a], zw.at[a], zring) for a in range(2)]
    def run(steps):
        act = {"B": begin, "W": widen, "F": fetch, "P": project}
        for step in steps.split():
            act[step[0]](*[int(v) for v in step[1:]])

    local[0].wait()
    run("B00 B01")
    twins = {}
    for a, i in ((0, 2), (1, 0), (1, 1), (1, 2), (0, 3), (1, 3)):
        if (a, i) == (1, 0):
            local[1].wait()
        mine = (X, G)[a].at[js[i], y, x, d]
        twins[a, i] = links.push(mine, mine, {"dp": 1 - d}, twin_send)
    for copy in local[2:]:
        copy.wait()
    w_swap = (links.push(win.at[1 - c], wino, core), links.push(wout.at[1 - c], wouto, core))
    run("B02 B10 W00 W01")
    links.recv(w_swap[0], wino)
    links.recv(w_swap[1], wouto)
    run("P000 P010 W02 W10 B11 B12 P020 P100")
    run("F001 F002 F011 F012 P001 P002 P011 P012")
    run("F021 F022 F003 P021 P022 F013 P003 P013")
    run("F101 F102 F023 W11 W12 B03 B13 P101 P102 P023 F103 P110 P120 P103")
    zred[0].combine()
    run("F111 F112 F121 F122 P111 P112 P121 P122 F113 F123 W03 W13 P113 P123")
    zred[1].combine()
    run("F031 F032 F131 F132 P030 P031 P032 F033 P033 F133")

    hidden = [
        Gather(links, lambda p: Act.at[c, p], zring, Act.at[c, pl.ds(0, 3)]),
        Gather(links, lambda p: Pg.at[c, p], zring, Pg.at[c, pl.ds(0, 3)]),
    ]
    spread, spread_send = [{}, {}], [links.sends(full.at[c]) for full in (Act, Pg)]

    blocks = (k, wrap(k + 3), wrap(k + 1), wrap(k + 2))

    def spread_to(a, b, h):
        mine = (Act, Pg)[a].at[c, blocks[b], :, :, h]
        spread[a][b, h] = links.push(mine, mine, core, spread_send[a])


    zred[0].arrive()

    @pl.loop(0, 16)
    def _(r):
        at = (lax.div(r, 4), lax.rem(r, 4))
        act, gain = gelu_parts(zred[0].total(*at))
        Act[(c, k, *at)] = act.astype(BF)
        slope[at] = gain

    spread_to(0, 0, 0)
    spread_to(0, 0, 1)
    hidden[0].start(0)
    hidden[0].start(1)
    run("P130 P131 P132 P133")
    zred[1].arrive()

    @pl.loop(0, 16)
    def _(r):
        at = (lax.div(r, 4), lax.rem(r, 4))
        Pg[(c, k, *at)] = (zred[1].total(*at) * slope[at]).astype(BF)

    spread_to(1, 0, 0)
    spread_to(1, 0, 1)
    hidden[1].start(0)

    plane = {}

    def parts(a, b):
        if b == 3:
            return [(3 + 4 * a, 0, slice(0, 256)), (8 + a, 1, slice(256, 512))]
        return [(4 * a + b, (a + b) % 2, slice(0, 512))]

    flows, flow_send = {}, links.sends(b1.at[pl.ds(0, 8), pl.ds(0, 3)])

    def late(a, b):
        return b == 3

    def emit(a, b, halves=(0, 1)):
        j = blocks[b]
        full = (Act, Pg)[a]
        for h in halves:
            links.recv(spread[a][b, h], full.at[1 - c, j, :, :, h])
            left = [full[e, j, :, :, h].reshape(256, 256) for e in range(2)]
            if a == 0:
                value = dot(left[0], wout[0], (1, 0)) + dot(left[1], wout[1], (1, 0))
            else:
                value = dot(left[0], win[0], (1, 1)) + dot(left[1], win[1], (1, 1))
            O[:, :, h] = value.reshape(4, 4, 16, 512)
        some = slice(0, 2) if len(halves) == 2 else slice(halves[0], halves[0] + 1)
        for n, turn, cols in parts(a, b):
            if n not in plane:
                plane[n] = (ydirect, xdirect)[turn](False)
                flows[n] = (flow_send, links.recvs())
            one = plane[n]
            for r in (2, 1, 3):
                p = wrap(one.p + r)
                piece = O[p, :, some, :, cols] if turn == 0 else O[:, p, some, :, cols]
                src, dst = [b1.at[n, s, :, some, :, cols] for s in (r - 1, r + 2)]
                src[...] = piece.astype(BF)
                one.push((r, 0), src, dst, *flows[n])
        for n, turn, cols in parts(a, b):
            p = plane[n].p
            w1[n, :, some, :, cols] = O[p, :, some, :, cols] if turn == 0 else O[:, p, some, :, cols]

    def narrow(a, b):
        for n, turn, cols in parts(a, b):
            one = plane[n]
            value = w1[n, :, :, :, cols]
            one.recv((2, 0), b1.at[n, pl.ds(3, 3), :, :, :, cols])
            for r in (1, 3, 2):
                value = value + b1[n, 2 + r, :, :, :, cols].astype(F32)
            O[0, :, :, :, cols] = value
            last = late(a, b)
            plane[n] = two = (xdirect, ydirect)[turn](last)
            send, recv = links.sends(b2.at[n, pl.ds(0, 7), 0, :, cols] if last else b2.at[n, pl.ds(0, 3)]), links.recvs()
            for r, dd in sorted(two.to, key=lambda key: (key[0] != 2, key)):
                p = wrap(two.p + r)
                if last:
                    s = 2 * r + dd - 1
                    src, dst = [b2.at[n, t, 0, :, cols] for t in (s, 7 + s)]
                    src[...] = O[0, p, d if dd == 0 else 1 - d, :, cols].astype(BF)
                else:
                    src, dst = b2.at[n, r - 1], b2.at[n, 2 + r]
                    src[...] = O[0, p].astype(BF)
                two.push((r, dd), src, dst, send, recv)
            w2[n, :, :, cols] = O[0, two.p, :, :, cols]

    def pair(a, b):
        ((n, turn, cols),) = parts(a, b)
        two = plane[n]
        value = w2[n]
        two.recv((2, 0), b2.at[n, pl.ds(3, 3)])
        for r in (1, 3, 2):
            value = value + b2[n, 2 + r].astype(F32)
        w2[n] = value
        b2[n, 6, 0] = w2[n, 1 - d].astype(BF)
        plane[n] = links.push(b2.at[n, 6, 0], b2.at[n, 7, 0], {"dp": 1 - d})

    def close(a, b):
        for n, turn, cols in parts(a, b):
            value = w2[n, d, :, cols]
            if late(a, b):
                plane[n].recv((2, 1), b2.at[n, pl.ds(7, 7), 0, :, cols])
                for t in range(7, 14):
                    value = value + b2[n, t, 0, :, cols].astype(F32)
            else:
                links.recv(plane[n], b2.at[n, 7, 0])
                value = value + b2[n, 7, 0].astype(F32)
            (out_o, gx_o)[a][blocks[b], :, cols] = value.astype(BF)

    def weights(a, b):
        j = blocks[b]
        for h in range(2):
            value = None
            for t in range(2):
                rows = pl.ds(2 * t, 2)
                hid = (Act, Pg)[a][h, j, rows].reshape(256, 256)
                wide = (G, X)[a][j, rows].reshape(256, 512)
                term = dot(hid, wide, (0, 0)) if a == 0 else dot(wide, hid, (0, 0))
                value = term if value is None else value + term
            acc = (acco, acci)[a]
            if b > 0:
                value = value + acc[h]
            if b < 3:
                acc[h] = value
            elif a == 0:
                gwo_o[h] = value.astype(BF)
            else:
                gwi_o[:, h * 256 : (h + 1) * 256] = value.astype(BF)

    def relay(a):
        hidden[a].relay()
        spread_to(a, 1, 0)
        spread_to(a, 2, 1)

    def sides(a):
        hidden[a].take(1)
        spread_to(a, 1, 1)
        spread_to(a, 2, 0)

    def finish(a):
        hidden[a].finish()
        spread_to(a, 3, 0)
        spread_to(a, 3, 1)

    emit(0, 0)
    emit(1, 0)
    weights(0, 0)
    relay(0)
    hidden[1].start(1)
    weights(1, 0)
    sides(0)
    emit(0, 1)
    emit(0, 2)
    relay(1)
    narrow(0, 0)
    narrow(1, 0)
    emit(1, 1, (0,))
    emit(1, 2, (1,))
    weights(0, 1)
    weights(0, 2)
    finish(0)
    emit(0, 3)
    narrow(0, 1)
    narrow(0, 2)
    weights(0, 3)
    sides(1)
    emit(1, 1, (1,))
    emit(1, 2, (0,))
    weights(1, 1)
    weights(1, 2)
    finish(1)
    emit(1, 3)
    narrow(0, 3)
    pair(0, 0)
    pair(1, 0)
    pair(0, 1)
    pair(0, 2)
    weights(1, 3)
    narrow(1, 1)
    narrow(1, 2)
    narrow(1, 3)
    pair(1, 1)
    pair(1, 2)
    close(0, 0), close(1, 0), close(0, 1), close(0, 2), close(0, 3)
    close(1, 1), close(1, 2)
    close(1, 3)
    links.drain()
    assert (len(links.sent), links.got) == (SENDS, RECVS), (len(links.sent), links.got)


def store(*refs):
    copies = [pltpu.make_async_copy(refs[i], refs[4 + i], refs[8].at[i]) for i in range(4)]
    for copy in copies:
        copy.start()
    for copy in copies:
        copy.wait()


def on_device(tokens, w_in, w_out, out_grad):
    any_spec = pl.BlockSpec(memory_space=pl.ANY)
    vmem = pl.BlockSpec(memory_space=pltpu.VMEM)
    full = pltpu.VMEM((4, 4, 4, 2, 16, 512), BF)
    hid = pltpu.VMEM((2, 4, 4, 4, 2, 16, 256), BF)
    results = pl.pallas_call(
        kernel,
        out_shape=(
            pltpu.VMEM((4, 16, 512), BF),
            pltpu.VMEM((4, 16, 512), BF),
            pltpu.VMEM((512, 512), BF),
            pltpu.VMEM((2, 256, 512), BF),
        ),
        in_specs=[any_spec] * 4,
        out_specs=(vmem,) * 4,
        scratch_shapes=[
            full, full, full, full,
            pltpu.VMEM((2, 512, 256), BF),
            pltpu.VMEM((512, 256), BF),
            pltpu.VMEM((2, 256, 512), BF),
            pltpu.VMEM((256, 512), BF),
            hid, hid,
            pltpu.VMEM((2, 6, 4, 4, 2, 16, 256), BF),
            pltpu.VMEM((2, 2, 4, 4, 16, 256), F32),
            pltpu.VMEM((2, 4, 4, 2, 16, 256), F32),
            pltpu.VMEM((4, 4, 2, 16, 256), F32),
            pltpu.VMEM((4, 4, 2, 16, 512), F32),
            pltpu.VMEM((10, 6, 4, 2, 16, 512), BF),
            pltpu.VMEM((10, 4, 2, 16, 512), F32),
            pltpu.VMEM((10, 14, 2, 16, 512), BF),
            pltpu.VMEM((10, 2, 16, 512), F32),
            pltpu.VMEM((2, 256, 512), F32),
            pltpu.VMEM((2, 512, 256), F32),
            pltpu.SemaphoreType.DMA((5,)),
            pltpu.SemaphoreType.DMA((SENDS,)),
            pltpu.SemaphoreType.DMA((RECVS,)),
        ],
        compiler_params=pltpu.CompilerParams(
            collective_id=0, has_side_effects=True, vmem_limit_bytes=58 << 20
        ),
        name="ffn",
    )(
        tokens.reshape(4, 16, 512),
        w_in,
        w_out.reshape(2, 2, 256, 512),
        out_grad.reshape(4, 16, 512),
    )
    results = [pltpu.with_memory_space_constraint(r, pltpu.VMEM) for r in results]
    output, grad_x, gw_in, gw_out = pl.pallas_call(
        store,
        out_shape=tuple(jax.ShapeDtypeStruct(r.shape, BF) for r in results),
        in_specs=[vmem] * 4,
        out_specs=(any_spec,) * 4,
        scratch_shapes=[pltpu.SemaphoreType.DMA((4,))],
        name="store",
    )(*results)
    return (
        output.reshape(64, 512),
        grad_x.reshape(64, 512),
        gw_in.reshape(512, 1, 512),
        gw_out.reshape(1, 512, 512),
    )


def solution(mesh):
    placed = (P(("dp", "col"), "row"), P("row", "col"), P("col", "row"), P(("dp", "col"), "row"))
    return jax.shard_map(
        on_device,
        mesh=mesh,
        in_specs=placed,
        out_specs=(
            P(("dp", "col"), "row"),
            P(("dp", "col"), "row"),
            P("row", "col", "dp"),
            P("col", "dp", "row"),
        ),
        check_vma=False,
    )
```

```python
import math

import jax
import jax.numpy as jnp
from jax import lax
from jax.experimental import pallas as pl
from jax.experimental.pallas import tpu as pltpu
from jax.sharding import PartitionSpec as P

F32, BF = jnp.float32, jnp.bfloat16
MESH = pl.DeviceIdType.MESH
SENDS, RECVS = 32, 130


def gelu_parts(pre):
    cdf = 0.5 * (1.0 + lax.erf(pre * (1.0 / math.sqrt(2.0))))
    pdf = jnp.exp(-0.5 * pre * pre) * (1.0 / math.sqrt(2.0 * math.pi))
    return pre * cdf, cdf + pre * pdf


def dot(left, right, dims):
    return lax.dot_general(left, right, ((dims[:1], dims[1:]), ((), ())), preferred_element_type=F32)


def wrap(p):
    return lax.rem(p, 4)


class Links:
    def __init__(self, ssem, rsem):
        self.ssem, self.rsem, self.sent, self.got, self.dev = ssem, rsem, [], 0, None

    def make(self, send, recv, src, dst, dev):
        return pltpu.make_async_remote_copy(
            src_ref=src,
            dst_ref=dst,
            send_sem=self.ssem.at[send],
            recv_sem=self.rsem.at[recv],
            device_id=dev,
            device_id_type=MESH,
        )

    def sends(self, total):
        self.sent.append(total)
        return len(self.sent) - 1

    def recvs(self):
        self.got += 1
        return self.got - 1

    def push(self, src, dst, dev, send=None, recv=None):
        send = self.sends(src) if send is None else send
        recv = self.recvs() if recv is None else recv
        self.make(send, recv, src, dst, dev).start()
        self.dev = dev
        return recv

    def recv(self, n, ref):
        self.make(0, n, ref, ref, self.dev).wait_recv()

    def drain(self):
        for n, total in enumerate(self.sent):
            self.make(n, 0, total, total, self.dev).wait_send()


def part(ref, half):
    n = ref.shape[0] // 2
    return ref.at[pl.ds(half * n, n)]


class Gather:
    def __init__(self, links, slot, ring, total):
        self.links, self.slot, (self.p, self.left, self.right) = links, slot, ring
        self.send, self.c, self.near = links.sends(total), links.recvs(), {}

    def start(self, second):
        mine = self.slot(self.p)
        near, far = mine.at[:, :, second], mine.at[:, :, 1 - second]
        self.near[second] = (
            self.links.push(near, near, self.right, self.send),
            self.links.push(far, far, self.left, self.send),
        )

    def take(self, second):
        left, right = [self.slot(wrap(self.p + n)).at[:, :, h] for n, h in ((3, second), (1, 1 - second))]
        self.links.recv(self.near[second][0], left)
        self.links.recv(self.near[second][1], right)
        return left, right

    def relay(self):
        left, right = self.take(0)
        self.links.push(left, left, self.right, self.send, self.c)
        self.links.push(right, right, self.left, self.send, self.c)

    def finish(self):
        self.links.recv(self.c, self.slot(wrap(self.p + 2)))


class Direct:
    def __init__(self, links, ring, col, dp, twins):
        self.links, self.p, self.sent = links, ring, {}
        self.to = {}
        for r in range(4):
            for dd in range(2 if twins else 1):
                if r + dd > 0:
                    dev = {"col": col(wrap(ring + r))}
                    if dd == 1:
                        dev = {"dp": 1 - dp} if r == 0 else {**dev, "dp": 1 - dp}
                    self.to[r, dd] = dev

    def push(self, key, src, dst, send, recv=None):
        self.sent[key] = self.links.push(src, dst, self.to[key], send, recv)

    def recv(self, key, ref):
        self.links.recv(self.sent[key], ref)


class Reduce:
    def __init__(self, links, bufs, keep, own, ring):
        self.links, (self.p, self.left, self.right) = links, ring
        self.so, self.sr, self.sl, self.ro, self.rl, self.rr = [bufs.at[i] for i in range(6)]
        self.kr, self.kl, self.own, self.both = keep.at[0], keep.at[1], own, bufs.at[pl.ds(4, 2)]
        self.send = links.sends(bufs.at[pl.ds(0, 3)])
        self.a, self.b, self.c = links.recvs(), links.recvs(), links.recvs()

    def put(self, i, at, value):
        push, half = self.links.push, [(*at, slice(None), h) if len(at) == 1 else (*at, h) for h in range(2)]
        if i == 0:
            self.so[at] = value.astype(BF)
            push(self.so.at[half[0]], self.ro.at[half[0]], self.right, self.send, self.a)
            push(self.so.at[half[1]], self.ro.at[half[1]], self.left, self.send, self.b)
        elif i == 1:
            self.sr[half[1]] = value[:, 1].astype(BF)
            push(self.sr.at[half[1]], self.rl.at[half[1]], self.right, self.send, self.c)
            self.kr[at] = value[:, 0]
        elif i == 2:
            self.sl[half[0]] = value[:, 0].astype(BF)
            push(self.sl.at[half[0]], self.rr.at[half[0]], self.left, self.send, self.c)
            self.kl[at] = value[:, 1]
        else:
            self.own[at] = value

    def combine(self):
        ways = (
            (self.a, self.sr, self.kr, self.rl, self.right),
            (self.b, self.sl, self.kl, self.rr, self.left),
        )
        for h, (sem, send, keep, to, dev) in enumerate(ways):
            self.links.recv(sem, self.ro.at[:, :, h])
            send[:, :, h] = (keep[...] + self.ro[:, :, h].astype(F32)).astype(BF)
            self.links.push(send.at[:, :, h], to.at[:, :, h], dev, self.send, self.c)

    def arrive(self):
        self.links.recv(self.c, self.both)

    def total(self, *at):
        return self.own[at] + self.rl[at].astype(F32) + self.rr[at].astype(F32)


def kernel(
    tok, w_in, w_out, og,
    out_o, gx_o, gwi_o, gwo_o,
    X, XO, G, GO, win, wino, wout, wouto,
    Act, Pg, zb, zk, zw, slope,
    O, b1, w1, b2, w2, acco, acci,
    lsem, ssem, rsem,
):
    d, row, col = lax.axis_index("dp"), lax.axis_index("row"), lax.axis_index("col")
    k, c = lax.div(row, 2), lax.rem(row, 2)
    y, x = lax.div(col, 4), lax.rem(col, 4)
    core = {"row": 2 * k + (1 - c)}
    zring = (k, {"row": 2 * wrap(k + 3) + c}, {"row": 2 * wrap(k + 1) + c})
    links = Links(ssem, rsem)

    def xdirect(twins):
        return Direct(links, x, lambda p: 4 * y + p, d, twins)

    def ydirect(twins):
        return Direct(links, y, lambda p: 4 * p + x, d, twins)

    local = [
        pltpu.make_async_copy(tok, X.at[:, y, x, d], lsem.at[0]),
        pltpu.make_async_copy(og, G.at[:, y, x, d], lsem.at[1]),
        pltpu.make_async_copy(w_out.at[d], wout, lsem.at[2]),
        pltpu.make_async_copy(w_in.at[:, pl.ds(pl.multiple_of(d * 512, 512), 256)], win.at[0], lsem.at[3]),
        pltpu.make_async_copy(w_in.at[:, pl.ds(pl.multiple_of(d * 512 + 256, 256), 256)], win.at[1], lsem.at[4]),
    ]
    for copy in local:
        copy.start()
    barrier = pltpu.get_barrier_semaphore()
    peers = [core, zring[1], zring[2], *xdirect(True).to.values()]
    peers += [dev for (r, _), dev in ydirect(True).to.items() if r > 0]
    for dev in peers:
        pl.semaphore_signal(barrier, inc=1, device_id=dev, device_id_type=MESH)
    pl.semaphore_wait(barrier, len(peers))

    js = (wrap(k + 2), wrap(k + 1), wrap(k + 3), k)
    first, second, shares = {}, {}, {}
    share_send = [links.sends(full) for full in (X, G)]
    ring_send = [links.sends(full.at[:, pl.ds(0, 3)]) for full in (X, G)]
    first_send = [links.sends(b2.at[pl.ds(0, 2), pl.ds(0, 7), 0]), links.sends(b2.at[pl.ds(0, 6), pl.ds(0, 3)])]
    twin_send = links.sends(b2.at[pl.ds(0, 6), 0, 0])

    def turn(a, i):
        return (a + i) % 2

    def slab(a, i, full, p):
        return (full.at[js[i], p], full.at[js[i], :, p])[turn(a, i)]

    def begin(a, i):
        both = a == 0 and i < 2
        first[a, i] = one = (xdirect, ydirect)[turn(a, i)](both)
        j, recv = js[i], links.recvs()
        if both:
            mine, send = (X, G)[a].at[j, y, x, d], first_send[0]
        else:
            links.recv(twins[a, i], (X, G)[a].at[j, y, x, 1 - d])
            mine, send = (X, G)[a].at[j, y, x], first_send[1]
        for key in sorted(one.to, key=lambda key: (key[0] == 2, key)):
            one.push(key, mine, mine, send, recv)

    def share(a, i, q):
        two = second[a, i]
        p = wrap(two.p + (0, 3, 1, 2)[q])
        full, other = ((X, XO), (G, GO))[a]
        shares[a, i, q] = (p, links.push(slab(a, i, full, p), slab(a, i, other, p), core, share_send[a]))

    def widen(a, i):
        full = (X, G)[a]
        both = a == 0 and i < 2
        first[a, i].recv((2, 0), b2.at[8, pl.ds(0, 7), 0] if both else b2.at[8, pl.ds(0, 3)])
        second[a, i] = two = (ydirect, xdirect)[turn(a, i)](False)
        share(a, i, 0)
        mine, two.send = slab(a, i, full, two.p), ring_send[a]
        for r in (1, 3):
            two.push((r, 0), mine, mine, two.send)
        two.sent[2, 0] = links.recvs()

    def fetch(a, i, q):
        two = second[a, i]
        r = (0, 1, 3, 2)[q]
        ref = slab(a, i, (X, G)[a], wrap(two.p + 4 - r))
        two.recv((r, 0), ref)
        if q < 3:
            half = part(ref, q - 1)
            links.push(half, half, two.to[r, 0], two.send, two.sent[2, 0])
        share(a, i, q)

    def project(a, i, q):
        p, sem = shares[a, i, q]
        full, other, near, far, dims = ((X, XO, win, wino, (1, 0)), (G, GO, wout, wouto, (1, 1)))[a]
        links.recv(sem, slab(a, i, other, p))
        value = dot(slab(a, i, full, p)[...].reshape(128, 512), near[c], dims) + dot(
            slab(a, i, other, p)[...].reshape(128, 512), far[...], dims
        )
        at = (p,) if turn(a, i) == 0 else (slice(None), p)
        zred[a].put(i, at, value.reshape(4, 2, 16, 256))

    zred = [Reduce(links, zb.at[a], zk.at[a], zw.at[a], zring) for a in range(2)]
    def run(*steps):
        act = {"B": begin, "W": widen, "F": fetch, "P": project}
        for step in steps:
            act[step[0]](*[int(v) for v in step[1:]])

    local[0].wait()
    run("B00", "B01")
    twins = {}
    for a, i in ((0, 2), (1, 0), (1, 1), (1, 2), (0, 3), (1, 3)):
        if (a, i) == (1, 0):
            local[1].wait()
        mine = (X, G)[a].at[js[i], y, x, d]
        twins[a, i] = links.push(mine, mine, {"dp": 1 - d}, twin_send)
    for copy in local[2:]:
        copy.wait()
    w_swap = (links.push(win.at[1 - c], wino, core), links.push(wout.at[1 - c], wouto, core))
    run("B02", "B10", "W00", "W01")
    links.recv(w_swap[0], wino)
    links.recv(w_swap[1], wouto)
    run("P000", "P010", "W02", "W10", "B11", "B12", "P020", "P100")
    run("F001", "F002", "F011", "F012", "P001", "P002", "P011", "P012")
    run("F021", "F022", "F003", "P021", "P022", "F013", "P003", "P013")
    run("F101", "F102", "F023", "W11", "W12", "B03", "B13", "P101", "P102", "P023", "F103", "P110", "P120", "P103")
    zred[0].combine()
    run("F111", "F112", "F121", "F122", "P111", "P112", "P121", "P122", "F113", "F123", "W03", "W13", "P113", "P123")
    zred[1].combine()
    run("F031", "F032", "F131", "F132", "P030", "P031", "P032", "F033", "P033", "F133")

    hidden = [
        Gather(links, lambda p: Act.at[c, p], zring, Act.at[c, pl.ds(0, 3)]),
        Gather(links, lambda p: Pg.at[c, p], zring, Pg.at[c, pl.ds(0, 3)]),
    ]
    spread, spread_send = [{}, {}], [links.sends(full.at[c]) for full in (Act, Pg)]

    blocks = (k, wrap(k + 3), wrap(k + 1), wrap(k + 2))

    def spread_to(a, b, h):
        mine = (Act, Pg)[a].at[c, blocks[b], :, :, h]
        spread[a][b, h] = links.push(mine, mine, core, spread_send[a])


    zred[0].arrive()

    @pl.loop(0, 16)
    def _(r):
        at = (lax.div(r, 4), lax.rem(r, 4))
        act, gain = gelu_parts(zred[0].total(*at))
        Act[(c, k, *at)] = act.astype(BF)
        slope[at] = gain

    spread_to(0, 0, 0)
    spread_to(0, 0, 1)
    hidden[0].start(0)
    hidden[0].start(1)
    run("P130", "P131", "P132", "P133")
    zred[1].arrive()

    @pl.loop(0, 16)
    def _(r):
        at = (lax.div(r, 4), lax.rem(r, 4))
        Pg[(c, k, *at)] = (zred[1].total(*at) * slope[at]).astype(BF)

    spread_to(1, 0, 0)
    spread_to(1, 0, 1)
    hidden[1].start(0)

    plane = {}

    def parts(a, b):
        if b == 3:
            return [(3 + 4 * a, 0, slice(0, 256)), (8 + a, 1, slice(256, 512))]
        return [(4 * a + b, (a + b) % 2, slice(0, 512))]

    flows, flow_send = {}, links.sends(b1.at[pl.ds(0, 8), pl.ds(0, 3)])

    def late(a, b):
        return b == 3

    def emit(a, b, halves=(0, 1)):
        j = blocks[b]
        full = (Act, Pg)[a]
        for h in halves:
            links.recv(spread[a][b, h], full.at[1 - c, j, :, :, h])
            left = [full[e, j, :, :, h].reshape(256, 256) for e in range(2)]
            if a == 0:
                value = dot(left[0], wout[0], (1, 0)) + dot(left[1], wout[1], (1, 0))
            else:
                value = dot(left[0], win[0], (1, 1)) + dot(left[1], win[1], (1, 1))
            O[:, :, h] = value.reshape(4, 4, 16, 512)
        some = slice(0, 2) if len(halves) == 2 else slice(halves[0], halves[0] + 1)
        for n, turn, cols in parts(a, b):
            if n not in plane:
                plane[n] = (ydirect, xdirect)[turn](False)
                flows[n] = (flow_send, links.recvs())
            one = plane[n]
            for r in (2, 1, 3):
                p = wrap(one.p + r)
                piece = O[p, :, some, :, cols] if turn == 0 else O[:, p, some, :, cols]
                src, dst = [b1.at[n, s, :, some, :, cols] for s in (r - 1, r + 2)]
                src[...] = piece.astype(BF)
                one.push((r, 0), src, dst, *flows[n])
        for n, turn, cols in parts(a, b):
            p = plane[n].p
            w1[n, :, some, :, cols] = O[p, :, some, :, cols] if turn == 0 else O[:, p, some, :, cols]

    def narrow(a, b):
        for n, turn, cols in parts(a, b):
            one = plane[n]
            value = w1[n, :, :, :, cols]
            one.recv((2, 0), b1.at[n, pl.ds(3, 3), :, :, :, cols])
            for r in (1, 3, 2):
                value = value + b1[n, 2 + r, :, :, :, cols].astype(F32)
            O[0, :, :, :, cols] = value
            last = late(a, b)
            plane[n] = two = (xdirect, ydirect)[turn](last)
            send, recv = links.sends(b2.at[n, pl.ds(0, 7), 0, :, cols] if last else b2.at[n, pl.ds(0, 3)]), links.recvs()
            for r, dd in sorted(two.to, key=lambda key: (key[0] != 2, key)):
                p = wrap(two.p + r)
                if last:
                    s = 2 * r + dd - 1
                    src, dst = [b2.at[n, t, 0, :, cols] for t in (s, 7 + s)]
                    src[...] = O[0, p, d if dd == 0 else 1 - d, :, cols].astype(BF)
                else:
                    src, dst = b2.at[n, r - 1], b2.at[n, 2 + r]
                    src[...] = O[0, p].astype(BF)
                two.push((r, dd), src, dst, send, recv)
            w2[n, :, :, cols] = O[0, two.p, :, :, cols]

    def pair(a, b):
        ((n, turn, cols),) = parts(a, b)
        two = plane[n]
        value = w2[n]
        two.recv((2, 0), b2.at[n, pl.ds(3, 3)])
        for r in (1, 3, 2):
            value = value + b2[n, 2 + r].astype(F32)
        w2[n] = value
        b2[n, 6, 0] = w2[n, 1 - d].astype(BF)
        plane[n] = links.push(b2.at[n, 6, 0], b2.at[n, 7, 0], {"dp": 1 - d})

    def close(a, b):
        for n, turn, cols in parts(a, b):
            value = w2[n, d, :, cols]
            if late(a, b):
                plane[n].recv((2, 1), b2.at[n, pl.ds(7, 7), 0, :, cols])
                for t in range(7, 14):
                    value = value + b2[n, t, 0, :, cols].astype(F32)
            else:
                links.recv(plane[n], b2.at[n, 7, 0])
                value = value + b2[n, 7, 0].astype(F32)
            (out_o, gx_o)[a][blocks[b], :, cols] = value.astype(BF)

    def weights(a, b):
        j = blocks[b]
        for h in range(2):
            value = None
            for t in range(2):
                rows = pl.ds(2 * t, 2)
                hid = (Act, Pg)[a][h, j, rows].reshape(256, 256)
                wide = (G, X)[a][j, rows].reshape(256, 512)
                term = dot(hid, wide, (0, 0)) if a == 0 else dot(wide, hid, (0, 0))
                value = term if value is None else value + term
            acc = (acco, acci)[a]
            if b > 0:
                value = value + acc[h]
            if b < 3:
                acc[h] = value
            elif a == 0:
                gwo_o[h] = value.astype(BF)
            else:
                gwi_o[:, h * 256 : (h + 1) * 256] = value.astype(BF)

    def relay(a):
        hidden[a].relay()
        spread_to(a, 1, 0)
        spread_to(a, 2, 1)

    def sides(a):
        hidden[a].take(1)
        spread_to(a, 1, 1)
        spread_to(a, 2, 0)

    def finish(a):
        hidden[a].finish()
        spread_to(a, 3, 0)
        spread_to(a, 3, 1)

    emit(0, 0)
    emit(1, 0)
    weights(0, 0)
    relay(0)
    hidden[1].start(1)
    weights(1, 0)
    sides(0)
    emit(0, 1)
    emit(0, 2)
    relay(1)
    narrow(0, 0)
    narrow(1, 0)
    emit(1, 1, (0,))
    emit(1, 2, (1,))
    weights(0, 1)
    weights(0, 2)
    finish(0)
    emit(0, 3)
    narrow(0, 1)
    narrow(0, 2)
    weights(0, 3)
    sides(1)
    emit(1, 1, (1,))
    emit(1, 2, (0,))
    weights(1, 1)
    weights(1, 2)
    finish(1)
    emit(1, 3)
    narrow(0, 3)
    pair(0, 0)
    pair(1, 0)
    pair(0, 1)
    pair(0, 2)
    weights(1, 3)
    narrow(1, 1)
    narrow(1, 2)
    narrow(1, 3)
    pair(1, 1)
    pair(1, 2)
    close(0, 0), close(1, 0), close(0, 1), close(0, 2), close(0, 3)
    close(1, 1), close(1, 2)
    close(1, 3)
    links.drain()
    assert (len(links.sent), links.got) == (SENDS, RECVS), (len(links.sent), links.got)


def store(*refs):
    copies = [pltpu.make_async_copy(refs[i], refs[4 + i], refs[8].at[i]) for i in range(4)]
    for copy in copies:
        copy.start()
    for copy in copies:
        copy.wait()


def on_device(tokens, w_in, w_out, out_grad):
    any_spec = pl.BlockSpec(memory_space=pl.ANY)
    vmem = pl.BlockSpec(memory_space=pltpu.VMEM)
    full = pltpu.VMEM((4, 4, 4, 2, 16, 512), BF)
    hid = pltpu.VMEM((2, 4, 4, 4, 2, 16, 256), BF)
    results = pl.pallas_call(
        kernel,
        out_shape=(
            pltpu.VMEM((4, 16, 512), BF),
            pltpu.VMEM((4, 16, 512), BF),
            pltpu.VMEM((512, 512), BF),
            pltpu.VMEM((2, 256, 512), BF),
        ),
        in_specs=[any_spec] * 4,
        out_specs=(vmem,) * 4,
        scratch_shapes=[
            full, full, full, full,
            pltpu.VMEM((2, 512, 256), BF),
            pltpu.VMEM((512, 256), BF),
            pltpu.VMEM((2, 256, 512), BF),
            pltpu.VMEM((256, 512), BF),
            hid, hid,
            pltpu.VMEM((2, 6, 4, 4, 2, 16, 256), BF),
            pltpu.VMEM((2, 2, 4, 4, 16, 256), F32),
            pltpu.VMEM((2, 4, 4, 2, 16, 256), F32),
            pltpu.VMEM((4, 4, 2, 16, 256), F32),
            pltpu.VMEM((4, 4, 2, 16, 512), F32),
            pltpu.VMEM((10, 6, 4, 2, 16, 512), BF),
            pltpu.VMEM((10, 4, 2, 16, 512), F32),
            pltpu.VMEM((10, 14, 2, 16, 512), BF),
            pltpu.VMEM((10, 2, 16, 512), F32),
            pltpu.VMEM((2, 256, 512), F32),
            pltpu.VMEM((2, 512, 256), F32),
            pltpu.SemaphoreType.DMA((5,)),
            pltpu.SemaphoreType.DMA((SENDS,)),
            pltpu.SemaphoreType.DMA((RECVS,)),
        ],
        compiler_params=pltpu.CompilerParams(
            collective_id=0, has_side_effects=True, vmem_limit_bytes=58 << 20
        ),
        name="ffn",
    )(
        tokens.reshape(4, 16, 512),
        w_in,
        w_out.reshape(2, 2, 256, 512),
        out_grad.reshape(4, 16, 512),
    )
    results = [pltpu.with_memory_space_constraint(r, pltpu.VMEM) for r in results]
    output, grad_x, gw_in, gw_out = pl.pallas_call(
        store,
        out_shape=tuple(jax.ShapeDtypeStruct(r.shape, BF) for r in results),
        in_specs=[vmem] * 4,
        out_specs=(any_spec,) * 4,
        scratch_shapes=[pltpu.SemaphoreType.DMA((4,))],
        name="store",
    )(*results)
    return (
        output.reshape(64, 512),
        grad_x.reshape(64, 512),
        gw_in.reshape(512, 1, 512),
        gw_out.reshape(1, 512, 512),
    )


def solution(mesh):
    placed = (P(("dp", "col"), "row"), P("row", "col"), P("col", "row"), P(("dp", "col"), "row"))
    return jax.shard_map(
        on_device,
        mesh=mesh,
        in_specs=placed,
        out_specs=(
            P(("dp", "col"), "row"),
            P(("dp", "col"), "row"),
            P("row", "col", "dp"),
            P("col", "dp", "row"),
        ),
        check_vma=False,
    )
```
